512 devices in a mesh: gx: 64 (over z, y), gz: 8 (over x, core).
Axes of the slice: x: 4, y: 4, z: 16, core: 2. Of those that a mesh axis runs over, the one named last changes fastest.
Arguments:
- tokens: bfloat16 [4, 256, 64, 768], P(None, 'gx', 'gz'), may hold values from -60 to 60
- cross_qkv: bfloat16 [768, 2304], P(None, 'gx'), may hold values from -16 to 16
- cross_out: bfloat16 [768, 768], P('gx'), may hold values from -0.21875 to 0.21875
- depth_qkv: bfloat16 [768, 2304], P(None, 'gx'), may hold values from -16 to 16
- depth_out: bfloat16 [768, 768], P('gx'), may hold values from -0.21875 to 0.21875
- up_proj: bfloat16 [768, 3072], P(None, 'gz'), may hold values from -0.21875 to 0.21875
- down_proj: bfloat16 [3072, 768], P('gz'), may hold values from -0.109375 to 0.109375
- gains: float32 [3, 768], replicated, may hold values from 0.5 to 1.5
- head_weight: float32 [768], replicated, may hold values from -0.21875 to 0.21875
- head_bias: float32 [1], replicated, may hold values from -1 to 1
Outputs:
- features: bfloat16 [4, 256, 64, 768], P(None, 'gx', 'gz')
- geotime: float32 [4, 256, 64], P(None, 'gx', 'gz')
The draws below stay inside these ranges and needn't reach their ends.
All inputs are finite; a program needn't handle non-finite values.
Results may differ from the reference program's by a relative error of at most 0.013.
Values may be sent and summed in bfloat16 or wider, within the bound.
A program may use at most 64 MiB of HBM per device.

```python
import math
import jax
import jax.numpy as jnp
from jax import lax

D = 768
HEADS = 12
HDIM = 64
FF = 3072
INL = 4
XL = 256
DP = 64
N_GZ = 8


def draw_tokens(key, part):
    base = jax.random.normal(key, (INL, XL, DP, D), jnp.float32)
    return jnp.clip(base, -60.0, 60.0).astype(jnp.bfloat16)


def projection_draw(key):
    columns = jax.random.normal(key, (D, 3 * D), jnp.float32) / math.sqrt(D)
    return jnp.clip(columns, -16.0, 16.0).astype(jnp.bfloat16)


def draw_cross_qkv(key, part):
    return projection_draw(jax.random.fold_in(key, 31))


def draw_depth_qkv(key, part):
    return projection_draw(jax.random.fold_in(key, 32))


def block_levels(key, shape, pieces, smallest, top_value):
    level, own = 1.0, jax.random.fold_in(key, 6)
    for axis_at, shards_of in pieces:
        steps = jnp.exp(jax.random.uniform(jax.random.fold_in(own, axis_at), (shards_of,), jnp.float32, smallest / len(pieces), top_value / len(pieces)))
        level = level * jnp.repeat(steps, shape[axis_at] // shards_of).reshape([-1 if axis == axis_at else 1 for axis in range(len(shape))])
    return level


def gaussian(stream_key, dims, scale, limit, shards=(), dtype=jnp.bfloat16):
    drawn = scale * jax.random.normal(stream_key, dims, jnp.float32)
    if shards:
        drawn = drawn * block_levels(stream_key, dims, shards, -0.22, 0.18)
    return jnp.clip(drawn, -limit, limit).astype(dtype)


def setup_inputs(seed: int = 0) -> dict:
    arg_keys = jax.random.split(jax.random.key(seed), 11)
    tokens = draw_tokens(jax.random.fold_in(arg_keys[10], 71), 0)
    cross_qkv = draw_cross_qkv(jax.random.fold_in(arg_keys[10], 71), 0)
    cross_out = gaussian(arg_keys[2], (D, D), D ** -0.5, 0.21875, ((0, 64),))
    depth_qkv = draw_depth_qkv(jax.random.fold_in(arg_keys[10], 71), 0)
    depth_out = gaussian(arg_keys[4], (D, D), D ** -0.5, 0.21875, ((0, 64),))
    up_proj = gaussian(arg_keys[5], (D, FF), D ** -0.5, 0.21875, ((1, 8),))
    down_proj = gaussian(arg_keys[6], (FF, D), FF ** -0.5, 0.109375, ((0, 8),))
    gains = jnp.clip(1.0 + 0.1 * jax.random.normal(arg_keys[7], (3, D), jnp.float32), 0.5, 1.5)
    head_weight = gaussian(arg_keys[8], (D,), D ** -0.5, 0.21875, (), jnp.float32)
    head_bias = jnp.clip(jax.random.uniform(arg_keys[9], (1,), jnp.float32, -1.0, 1.0), -1.0, 1.0)
    return {"tokens": tokens, "cross_qkv": cross_qkv, "cross_out": cross_out, "depth_qkv": depth_qkv, "depth_out": depth_out, "up_proj": up_proj, "down_proj": down_proj, "gains": gains, "head_weight": head_weight, "head_bias": head_bias}


log_span = math.log(256.0)

def encodings(inlines, crosslines, depths, cross_start, depth_start, model_width):
    pairs = model_width // 2
    index = jnp.arange(pairs)
    freq = math.pi * jnp.exp(-log_span * index.astype(jnp.float32) / pairs)
    which = index % 3
    inline_pos = jnp.arange(inlines).astype(jnp.float32)[:, None, None, None]
    cross_pos = (cross_start + jnp.arange(crosslines)).astype(jnp.float32)[None, :, None, None]
    depth_pos = (depth_start + jnp.arange(depths)).astype(jnp.float32)[None, None, :, None]
    zeros = jnp.zeros((inlines, crosslines, depths, pairs), jnp.float32)
    position = jnp.where(which == 0, inline_pos + zeros, jnp.where(which == 1, cross_pos + zeros, depth_pos + zeros))
    angle = position * freq
    return jnp.stack([jnp.sin(angle), jnp.cos(angle)], -1).reshape(inlines, crosslines, depths, model_width)

def normalize(stream, gain):
    scale = lax.rsqrt(lax.optimization_barrier(jnp.mean(stream * stream, -1, keepdims=True)) + 1e-05)
    return (stream * scale * gain).astype(jnp.bfloat16)

def attend(queries, keys, values):
    scale = queries.shape[-1] ** (-0.5)
    scores = jnp.einsum('...qe,...ke->...qk', queries.astype(jnp.float32), keys.astype(jnp.float32)) * scale
    scores = scores - lax.optimization_barrier(jnp.max(scores, -1, keepdims=True))
    expo = jnp.exp(scores)
    weights = (expo / lax.optimization_barrier(jnp.sum(expo, -1, keepdims=True))).astype(jnp.bfloat16)
    mixed = jnp.einsum('...qk,...ke->...qe', weights.astype(jnp.float32), values.astype(jnp.float32))
    return mixed.astype(jnp.bfloat16)

def reference(tokens, cross_qkv, cross_out, depth_qkv, depth_out, up_proj, down_proj, gains, head_weight, head_bias):
    count = INL * XL * DP
    stream = (tokens.astype(jnp.float32) + encodings(INL, XL, DP, 0, 0, D)).reshape(count, D)
    normed = normalize(stream, gains[0])
    packed = jnp.dot(normed, cross_qkv, preferred_element_type=jnp.float32).astype(jnp.bfloat16)
    packed = packed.reshape(INL, XL, DP, 3, HEADS, HDIM)
    lined = jnp.transpose(packed, (3, 0, 2, 4, 1, 5)).reshape(3, INL * DP, HEADS, XL, HDIM)
    mixed = lax.map(lambda trio: attend(trio[0], trio[1], trio[2]), (lined[0], lined[1], lined[2]))
    mixed = jnp.transpose(mixed.reshape(INL, DP, HEADS, XL, HDIM), (0, 3, 1, 2, 4)).reshape(count, D)
    stream = stream + jnp.dot(mixed, cross_out, preferred_element_type=jnp.float32)
    normed = normalize(stream, gains[1])
    packed = jnp.dot(normed, depth_qkv, preferred_element_type=jnp.float32).astype(jnp.bfloat16)
    packed = packed.reshape(INL, XL, DP, 3, HEADS, HDIM)
    lined = jnp.transpose(packed, (3, 0, 1, 4, 2, 5))
    mixed = lax.map(lambda trio: attend(trio[0], trio[1], trio[2]), (lined[0], lined[1], lined[2]))
    mixed = jnp.transpose(mixed, (0, 1, 3, 2, 4)).reshape(count, D)
    stream = stream + jnp.dot(mixed, depth_out, preferred_element_type=jnp.float32)
    normed = normalize(stream, gains[2])
    hidden = jax.nn.gelu(jnp.dot(normed, up_proj, preferred_element_type=jnp.float32)).astype(jnp.bfloat16)
    group = FF // N_GZ
    mlp_sum = jnp.zeros((count, D), jnp.float32)
    for member in range(N_GZ):
        partial_sum = jnp.dot(hidden[:, member * group:(member + 1) * group], down_proj[member * group:(member + 1) * group], preferred_element_type=jnp.float32)
        rounded = lax.optimization_barrier(partial_sum.astype(jnp.bfloat16))
        mlp_sum = mlp_sum + rounded.astype(jnp.float32)
    stream = stream + mlp_sum
    features = stream.astype(jnp.bfloat16).reshape(INL, XL, DP, D)
    thickness = jax.nn.softplus(jnp.dot(stream, head_weight, precision=lax.Precision.HIGHEST) + head_bias[0])
    geotime = jnp.cumsum(thickness.reshape(INL, XL, DP), axis=2)
    return (features, geotime)
```

```python
import functools
import math

import jax
import jax.numpy as jnp
import numpy as np
from jax import lax
from jax.experimental import pallas as pl
from jax.experimental.pallas import tpu as pltpu
from jax.sharding import PartitionSpec as P

ZN, YN, XN = 16, 4, 4
GX, GZ = ZN * YN, XN * 2
D, HEADS, HDIM, FF = 768, 12, 64, 3072
HALF = D // 2
INL, XL, DP = 4, 256, 64
XLD, DPD = XL // GX, DP // GZ
LINES = INL * DPD
MINE = 2 * DP
QKV_ROWS, OUT_ROWS = 144, 48
BLOCK = 2 * (QKV_ROWS + OUT_ROWS)
PIECE = 48
SLOT = 112
MESH = pl.DeviceIdType.MESH
BF, F32 = jnp.bfloat16, jnp.float32
ANY = pl.BlockSpec(memory_space=pl.ANY)
VM = pl.BlockSpec(memory_space=pltpu.VMEM)
LIMIT = 56 << 20


def table():
    k = np.arange(D // 2)
    freq = math.pi * np.exp(-math.log(256.0) * k / (D // 2))
    angle = np.arange(XL)[:, None] * freq[None, :]
    return np.stack([np.sin(angle), np.cos(angle)], -1).reshape(XL, D).astype(np.float32)


def packing():
    one = np.zeros((BLOCK, YN * SLOT), np.float32)
    row = 0
    for at, count in ((0, 36), (40, 12), (56, 36), (96, 12)):
        for y in range(YN):
            for r in range(count):
                one[row, y * SLOT + at + r] = 1
                row += 1
    return one


def place():
    gx, gz = lax.axis_index("gx"), lax.axis_index("gz")
    return gx, gz, gx // YN, gx % YN, gz // 2, gz % 2


def rcopy(src, dst, send, recv, gx, gz):
    return pltpu.make_async_remote_copy(
        src_ref=src, dst_ref=dst, send_sem=send, recv_sem=recv, device_id=(gx, gz), device_id_type=MESH
    )


def signal(gx, gz):
    pl.semaphore_signal(
        pltpu.get_barrier_semaphore(), inc=1, device_id=(gx, gz), device_id_type=MESH
    )


def gather_kernel(
    s_ref, t_ref, col_ref, one_ref, lines, cols, w, ybuf, block,
    y_s, y_r, t_s, t_r, c_s, c_r, z_s, z_r, p_s, p_r, b_s, b_r, l_s,
):
    gx, gz, z, y, x, c = place()
    half = gx // 32
    own_line = half == c
    for d in range(1, 4):
        signal(z * YN + (y + d) % YN, gz)
        signal(gx, ((x + d) % XN) * 2 + c)
    signal(((z + 1) % ZN) * YN + y, gz)
    signal(((z + 15) % ZN) * YN + y, gz)
    for d in range(1, 8):
        signal(gx, (gz + d) % GZ)

    def greet(i, _):
        there = 32 * c + i

        @pl.when(jnp.logical_or(there != gx, half != c))
        def _():
            signal(there, 2 * x + half)

        return 0

    lax.fori_loop(0, 32, greet, 0)
    pl.semaphore_wait(
        pltpu.get_barrier_semaphore(), 15 + 32 - jnp.where(own_line, 1, 0)
    )

    def y_copy(d):
        return rcopy(
            s_ref.at[c], ybuf.at[y], y_s.at[d - 1], y_r.at[d - 1], z * YN + (y + d) % YN, gz
        )

    own_y = pltpu.make_async_copy(s_ref.at[c], ybuf.at[y], l_s.at[0])
    own_y.start()
    for d in range(1, 4):
        y_copy(d).start()

    def t_copy(i):
        return rcopy(t_ref.at[i], lines.at[gx], t_s.at[i], t_r, 32 * c + i, 2 * x + half)

    def t_start(i, _):
        here = jnp.logical_and(32 * c + i == gx, own_line)

        @pl.when(jnp.logical_not(here))
        def _():
            t_copy(i).start()

        @pl.when(here)
        def _():
            pltpu.make_async_copy(t_ref.at[i], lines.at[gx], t_r).start()

        return 0

    lax.fori_loop(0, 32, t_start, 0)

    def c_copy(d):
        there = (gz + d) % GZ
        return rcopy(
            col_ref.at[there], cols.at[gz], c_s.at[d - 1], c_r.at[d - 1], gx, there
        )

    own_c = pltpu.make_async_copy(col_ref.at[gz], cols.at[gz], l_s.at[1])
    own_c.start()
    for d in range(1, 8):
        c_copy(d).start()

    own_y.wait()
    for d in range(1, 4):
        y_copy(d).wait_recv()
    block[...] = jnp.dot(
        one_ref[...], ybuf[...].reshape(YN * SLOT, HALF), preferred_element_type=F32
    ).astype(BF)
    own_w = pltpu.make_async_copy(block, w.at[c, z], l_s.at[2])
    own_w.start()

    rows = (pl.multiple_of(PIECE * y, 16), pl.multiple_of(BLOCK // 2 + PIECE * x, 16))

    def ring(way, s, first=False):
        back = s - 1
        zsrc = (z + jnp.where(way == 0, ZN - back, back)) % ZN
        znext = (z + (1 if way == 0 else ZN - 1)) % ZN
        return [
            rcopy(
                block.at[pl.ds(r, PIECE)] if first else w.at[c, zsrc, pl.ds(r, PIECE)],
                w.at[c, zsrc, pl.ds(r, PIECE)],
                z_s.at[way, s - 1, k],
                z_r.at[way, s - 1, k],
                znext * YN + y,
                gz,
            )
            for k, r in enumerate(rows)
        ]

    def arrived(way, s):
        zsrc = (z + (ZN - s if way == 0 else s)) % ZN
        for k, r in enumerate(rows):
            here = w.at[c, zsrc, pl.ds(r, PIECE)]
            rcopy(here, here, z_s.at[way, s - 1, k], z_r.at[way, s - 1, k], gx, gz).wait_recv()
        return zsrc

    def spread(zsrc):
        out = []
        for d in range(1, 4):
            for k, (tx, tz) in enumerate(
                ((z * YN + (y + d) % YN, gz), (gx, ((x + d) % XN) * 2 + c))
            ):
                piece = w.at[c, zsrc, pl.ds(rows[k], PIECE)]
                n = 2 * (d - 1) + k
                out.append(rcopy(piece, piece, p_s.at[zsrc, n], p_r.at[zsrc, n], tx, tz))
        return out

    def relay(zsrc):
        return rcopy(
            w.at[c, zsrc], w.at[c, zsrc], b_s.at[zsrc], b_r.at[zsrc], gx, 2 * x + 1 - c
        )

    def collect(zsrc):
        for d in range(1, 4):
            for k, r in enumerate(
                (PIECE * ((y + YN - d) % YN), BLOCK // 2 + PIECE * ((x + XN - d) % XN))
            ):
                n = 2 * (d - 1) + k
                here = w.at[c, zsrc, pl.ds(pl.multiple_of(r, 16), PIECE)]
                rcopy(here, here, p_s.at[zsrc, n], p_r.at[zsrc, n], gx, gz).wait_recv()
        relay(zsrc).start()

    for way in range(2):
        for cp in ring(way, 1, True):
            cp.start()
    own_w.wait()
    relay(z).start()

    def l_copy():
        mine = lines.at[pl.ds(pl.multiple_of(32 * c, 32), 32)]
        return rcopy(mine, mine, b_s.at[ZN], b_r.at[ZN], gx, 2 * x + 1 - c)

    def step(s, _):
        zsrc = arrived(0, s)

        @pl.when(s < 8)
        def _():
            for cp in ring(0, s + 1):
                cp.start()

        for cp in spread(zsrc):
            cp.start()

        @pl.when(s < 8)
        def _():
            zsrc = arrived(1, s)

            @pl.when(s < 7)
            def _():
                for cp in ring(1, s + 1):
                    cp.start()

            for cp in spread(zsrc):
                cp.start()

        @pl.when(s > 1)
        def _():
            collect((z + ZN - s + 1) % ZN)
            collect((z + s - 1) % ZN)

        @pl.when(s == 5)
        def _():
            mine = lines.at[pl.ds(pl.multiple_of(32 * c, 32), 32)]
            pltpu.make_async_copy(mine, mine, t_r).wait()
            l_copy().start()

        return 0

    lax.fori_loop(1, 9, step, 0)
    collect((z + 8) % ZN)

    for d in range(1, 8):
        c_copy(d).wait_recv()
        c_copy(d).wait_send()
    own_c.wait()
    for d in range(1, 4):
        y_copy(d).wait_send()

    def t_end(i, _):
        @pl.when(jnp.logical_not(jnp.logical_and(32 * c + i == gx, own_line)))
        def _():
            t_copy(i).wait_send()

        return 0

    lax.fori_loop(0, 32, t_end, 0)
    theirs = lines.at[pl.ds(pl.multiple_of(32 * (1 - c), 32), 32)]
    rcopy(theirs, theirs, b_s.at[ZN], b_r.at[ZN], gx, gz).wait_recv()
    l_copy().wait_send()
    for way in range(2):
        for cp in ring(way, 1, True):
            cp.wait_send()

    def r_end(s, _):
        for cp in ring(0, s):
            cp.wait_send()

        @pl.when(s < 8)
        def _():
            for cp in ring(1, s):
                cp.wait_send()

        return 0

    lax.fori_loop(2, 9, r_end, 0)

    def w_end(k, _):
        zsrc = (z + k) % ZN

        @pl.when(k > 0)
        def _():
            for cp in spread(zsrc):
                cp.wait_send()

        theirs = w.at[1 - c, zsrc]
        rcopy(theirs, theirs, b_s.at[zsrc], b_r.at[zsrc], gx, gz).wait_recv()
        relay(zsrc).wait_send()
        return 0

    lax.fori_loop(0, ZN, w_end, 0)


def gather(shards, lines, cols):
    dma = pltpu.SemaphoreType.DMA
    return pl.pallas_call(
        gather_kernel,
        out_shape=(
            jax.ShapeDtypeStruct((GX, XLD, D), BF),
            jax.ShapeDtypeStruct((GZ, 2 * DPD, D), BF),
            jax.ShapeDtypeStruct((2, ZN, BLOCK, HALF), BF),
        ),
        in_specs=[ANY, ANY, ANY, VM],
        out_specs=(ANY, ANY, ANY),
        scratch_shapes=[
            pltpu.VMEM((YN, SLOT, HALF), BF),
            pltpu.VMEM((BLOCK, HALF), BF),
            dma((3,)), dma((3,)),
            dma((32,)), dma,
            dma((7,)), dma((7,)),
            dma((2, 8, 2)), dma((2, 8, 2)),
            dma((ZN, 6)), dma((ZN, 6)),
            dma((ZN + 1,)), dma((ZN + 1,)),
            dma((3,)),
        ],
        compiler_params=pltpu.CompilerParams(
            collective_id=0, has_side_effects=True, vmem_limit_bytes=LIMIT
        ),
        name="gather",
    )(shards, lines, cols, jnp.asarray(packing(), BF))


def nt(a, b):
    return lax.dot_general(a, b, (((1,), (1,)), ((), ())), preferred_element_type=F32)


def normed(stream, gain):
    scale = lax.rsqrt(jnp.mean(stream * stream, -1, keepdims=True) + 1e-05)
    return (stream * scale * gain).astype(BF)


def which_axis(shape):
    return (lax.broadcasted_iota(jnp.int32, shape, 1) // 2) % 3


def attend(wq, keys_in, queries_in, kbuf, qbuf, vbuf, obuf, mask):
    def project(rows, tokens, left):
        a, b = wq[0, rows, :], wq[1, rows, :]
        lo, hi = tokens[:, :HALF], tokens[:, HALF:]
        return (nt(a, lo) + nt(b, hi) if left else nt(lo, a) + nt(hi, b)).astype(BF)

    qbuf[...] = project(slice(0, D), queries_in, True)
    kbuf[...] = project(slice(D, 2 * D), keys_in, False)
    vbuf[...] = project(slice(2 * D, 3 * D), keys_in, True)
    for h in range(HEADS):
        at = slice(h * HDIM, (h + 1) * HDIM)
        scores = jnp.dot(kbuf[:, at], qbuf[at, :], preferred_element_type=F32) * (HDIM**-0.5)
        if mask is not None:
            scores = jnp.where(mask, scores, -1e30)
        expo = jnp.exp(scores - jnp.max(scores, 0, keepdims=True))
        total = jnp.sum(expo, 0, keepdims=True)
        mixed = jnp.dot(vbuf[at, :], expo.astype(BF), preferred_element_type=F32)
        obuf[at, :] = mixed / total


def line_kernel(tok, enc, gain, w, out, wq, kbuf, qbuf, vbuf, obuf, sem):
    gx, gz, _, _, x, c = place()
    load = pltpu.make_async_copy(w.at[:, :, pl.ds(0, QKV_ROWS), :], wq, sem)
    load.start()
    inl = (gx % 32) // 8
    dep = DPD * (2 * x + gx // 32) + gx % 8
    which = which_axis((XL, D))
    pos = jnp.where(
        which == 1, enc[...], jnp.where(which == 0, enc[pl.ds(inl, 1), :], enc[pl.ds(dep, 1), :])
    )
    n = normed(tok[...].astype(F32) + pos, gain[...])
    q = lax.broadcasted_iota(jnp.int32, (MINE, XL), 0)
    r = lax.broadcasted_iota(jnp.int32, (MINE, XL), 1)
    pick = jnp.where(r == 4 * (q // 2) + 2 * c + q % 2, 1.0, 0.0).astype(BF)
    mine = jnp.dot(pick, n, preferred_element_type=F32).astype(BF)
    load.wait()
    attend(wq.reshape(2, 3 * D, HALF), n, mine, kbuf, qbuf, vbuf, obuf, None)
    out[...] = obuf[...].T.astype(BF)


def line_attention(tok, enc, gain, w):
    return pl.pallas_call(
        line_kernel,
        out_shape=jax.ShapeDtypeStruct((MINE, D), BF),
        in_specs=[VM, VM, VM, ANY],
        out_specs=VM,
        scratch_shapes=[
            pltpu.VMEM((2, ZN, QKV_ROWS, HALF), BF),
            pltpu.VMEM((XL, D), BF),
            pltpu.VMEM((D, MINE), BF),
            pltpu.VMEM((D, XL), BF),
            pltpu.VMEM((D, MINE), F32),
            pltpu.SemaphoreType.DMA,
        ],
        compiler_params=pltpu.CompilerParams(vmem_limit_bytes=LIMIT),
        name="line_attention",
    )(tok, enc, gain, w)


def back_kernel(mixed, out, s_sem, r_sem):
    gx, gz, _, _, x, c = place()
    inl = (gx % 32) // 8
    dep = DPD * (2 * x + gx // 32) + gx % 8
    me_too = inl == x

    def greet(i, _):
        there, other = 32 * ((i // 8) % 2) + 8 * x + i % 8, 2 * (i // 16) + c

        @pl.when(jnp.logical_or(there != gx, other != gz))
        def _():
            signal(there, other)

        return 0

    lax.fori_loop(0, 64, greet, 0)
    pl.semaphore_wait(pltpu.get_barrier_semaphore(), 64 - jnp.where(me_too, 1, 0))

    def copy(i):
        return rcopy(mixed.at[i], out.at[dep], s_sem.at[i], r_sem, i, 2 * inl + c)

    def start(i, _):
        here = jnp.logical_and(i == gx, me_too)

        @pl.when(jnp.logical_not(here))
        def _():
            copy(i).start()

        @pl.when(here)
        def _():
            pltpu.make_async_copy(mixed.at[i], out.at[dep], r_sem).start()

        return 0

    lax.fori_loop(0, 64, start, 0)
    pltpu.make_async_copy(out, out, r_sem).wait()

    def end(i, _):
        @pl.when(jnp.logical_not(jnp.logical_and(i == gx, me_too)))
        def _():
            copy(i).wait_send()

        return 0

    lax.fori_loop(0, 64, end, 0)


def back(mixed):
    return pl.pallas_call(
        back_kernel,
        out_shape=jax.ShapeDtypeStruct((DP, 2, D), BF),
        in_specs=[ANY],
        out_specs=ANY,
        scratch_shapes=[pltpu.SemaphoreType.DMA((64,)), pltpu.SemaphoreType.DMA],
        compiler_params=pltpu.CompilerParams(collective_id=1, has_side_effects=True),
        name="back",
    )(mixed)


def column_kernel(
    mixed, cols, enc, dep2, gains, w, stream_out, normed_out,
    w2, wq, w4, kbuf, qbuf, vbuf, obuf, sem,
):
    gx, _, _, _, x, c = place()
    parts = (0, QKV_ROWS), (QKV_ROWS, OUT_ROWS), (BLOCK // 2, QKV_ROWS), (BLOCK // 2 + QKV_ROWS, OUT_ROWS)
    loads = [
        pltpu.make_async_copy(w.at[:, :, pl.ds(*parts[k]), :], to, sem.at[k - 1])
        for k, to in ((1, w2), (2, wq), (3, w4))
    ]
    for load in loads:
        load.start()
    which = which_axis((MINE, D))
    odd = lax.broadcasted_iota(jnp.int32, (MINE, D), 0) % 2
    first = XLD * gx + 2 * c
    cross = jnp.where(odd == 0, enc[pl.ds(first, 1), :], enc[pl.ds(first + 1, 1), :])
    pos = jnp.where(which == 1, cross, jnp.where(which == 0, enc[pl.ds(x, 1), :], dep2[...]))
    stream = cols[...].astype(F32) + pos

    def project(v, wo):
        return jnp.concatenate(
            [
                jnp.dot(v, wo[k].reshape(D, HALF), preferred_element_type=F32)
                for k in range(2)
            ],
            1,
        )

    loads[0].wait()
    stream = stream + project(mixed[...], w2)
    n = normed(stream, gains[1:2, :])
    mask = (
        lax.broadcasted_iota(jnp.int32, (MINE, MINE), 0)
        + lax.broadcasted_iota(jnp.int32, (MINE, MINE), 1)
    ) % 2 == 0
    loads[1].wait()
    attend(wq.reshape(2, 3 * D, HALF), n, n, kbuf, qbuf, vbuf, obuf, mask)
    loads[2].wait()
    stream = stream + project(obuf[...].T.astype(BF), w4)
    stream_out[...] = stream
    normed_out[...] = normed(stream, gains[2:3, :])


def column_attention(mixed, cols, enc, dep2, gains, w):
    return pl.pallas_call(
        column_kernel,
        out_shape=(
            jax.ShapeDtypeStruct((MINE, D), F32),
            jax.ShapeDtypeStruct((MINE, D), BF),
        ),
        in_specs=[VM, VM, VM, VM, VM, ANY],
        out_specs=(VM, VM),
        scratch_shapes=[
            pltpu.VMEM((2, ZN, OUT_ROWS, HALF), BF),
            pltpu.VMEM((2, ZN, QKV_ROWS, HALF), BF),
            pltpu.VMEM((2, ZN, OUT_ROWS, HALF), BF),
            pltpu.VMEM((MINE, D), BF),
            pltpu.VMEM((D, MINE), BF),
            pltpu.VMEM((D, MINE), BF),
            pltpu.VMEM((D, MINE), F32),
            pltpu.SemaphoreType.DMA((3,)),
        ],
        compiler_params=pltpu.CompilerParams(vmem_limit_bytes=LIMIT),
        name="column_attention",
    )(mixed, cols, enc, dep2, gains, w)


def mlp_kernel(
    n_ref, stream, up, down, head_w, head_b, feat, time,
    tokens, sent, pair, sums, got, fbuf, gbuf,
    g_s, g_r, b_s, b_r, q_s, q_r, s_s, s_r, f_s, f_r, h_s, h_r, l_s,
):
    gx, gz, _, _, x, c = place()
    sib = 2 * x + 1 - c
    for d in range(1, 8):
        signal(gx, (gz + d) % GZ)
    pl.semaphore_wait(pltpu.get_barrier_semaphore(), 7)

    def to_chip(d):
        return rcopy(n_ref, tokens.at[d, c], g_s.at[d - 1], g_r.at[d - 1], gx, ((x + d) % XN) * 2 + c)

    def to_sib(d):
        src = n_ref if d == 0 else tokens.at[d, c]
        return rcopy(src, tokens.at[d, c], b_s.at[d], b_r.at[d], gx, sib)

    order = (1, 3, 2)
    for d in order:
        to_chip(d).start()
    to_sib(0).start()
    own = pltpu.make_async_copy(n_ref, tokens.at[0, c], l_s.at[0])
    own.start()

    def from_sib(d):
        here = tokens.at[d, 1 - c]
        return rcopy(here, here, b_s.at[d], b_r.at[d], gx, sib)

    def pair_copy(d):
        return rcopy(sent.at[d, 1 - c], pair.at[d], q_s.at[d], q_r.at[d], gx, sib)

    def home(d):
        return rcopy(
            sums.at[d], got.at[d - 1], s_s.at[d - 1], s_r.at[d - 1], gx, ((x + XN - d) % XN) * 2 + c
        )

    def finish(d):
        pair_copy(d).wait_recv()
        both = sent[d, c].astype(F32) + pair[d].astype(F32)
        if d == 0:
            return both
        sums[d] = both.astype(BF)
        home(d).start()
        return None

    def hidden_part(d):
        rows = tokens[d].reshape(2 * MINE, D)
        hidden = jax.nn.gelu(jnp.dot(rows, up[...], preferred_element_type=F32)).astype(BF)
        part = jnp.dot(hidden, down[...], preferred_element_type=F32).astype(BF)
        sent[d] = part.reshape(2, MINE, D)
        pair_copy(d).start()

    own.wait()
    from_sib(0).wait_recv()
    hidden_part(0)
    last = 0
    for d in order:
        to_chip(d).wait_recv()
        to_sib(d).start()
        from_sib(d).wait_recv()
        hidden_part(d)
        if last:
            finish(last)
        last = d
    finish(last)
    total = finish(0)
    for d in order:
        home(d).wait_recv()
        total = total + got[d - 1].astype(F32)
    stream3 = stream[...] + total
    fbuf[...] = stream3.astype(BF)
    thick = jax.nn.softplus(jnp.sum(stream3 * head_w[...], -1, keepdims=True) + head_b[0, 0])
    i = lax.broadcasted_iota(jnp.int32, (MINE, MINE), 0)
    j = lax.broadcasted_iota(jnp.int32, (MINE, MINE), 1)
    keep = jnp.logical_and(i <= j, (i + j) % 2 == 0)
    line = jnp.sum(jnp.where(keep, thick, 0.0), 0, keepdims=True)
    gbuf[...] = jnp.broadcast_to(line, (8, MINE))

    def f_copy(d):
        there = (gz + d) % GZ
        rows = fbuf.at[pl.ds(pl.multiple_of(16 * there, 16), 16)]
        return rcopy(rows, feat.at[gz], f_s.at[d - 1], f_r.at[d - 1], gx, there)

    def h_copy(d):
        return rcopy(gbuf, time.at[gz], h_s.at[d - 1], h_r.at[d - 1], gx, (gz + d) % GZ)

    for d in range(1, 8):
        f_copy(d).start()
        h_copy(d).start()
    own_f = pltpu.make_async_copy(fbuf.at[pl.ds(pl.multiple_of(16 * gz, 16), 16)], feat.at[gz], l_s.at[1])
    own_h = pltpu.make_async_copy(gbuf, time.at[gz], l_s.at[2])
    own_f.start()
    own_h.start()
    for d in range(1, 8):
        f_copy(d).wait()
        h_copy(d).wait()
    own_f.wait()
    own_h.wait()
    for d in range(1, 4):
        to_chip(d).wait_send()
        home(d).wait_send()
    for d in range(4):
        to_sib(d).wait_send()
        pair_copy(d).wait_send()


def mlp(n, stream, up, down, head_w, head_b):
    dma = pltpu.SemaphoreType.DMA
    return pl.pallas_call(
        mlp_kernel,
        out_shape=(
            jax.ShapeDtypeStruct((GZ, 16, D), BF),
            jax.ShapeDtypeStruct((GZ, 8, MINE), F32),
        ),
        in_specs=[VM, VM, VM, VM, VM, pl.BlockSpec(memory_space=pltpu.SMEM)],
        out_specs=(ANY, ANY),
        scratch_shapes=[
            pltpu.VMEM((4, 2, MINE, D), BF),
            pltpu.VMEM((4, 2, MINE, D), BF),
            pltpu.VMEM((4, MINE, D), BF),
            pltpu.VMEM((4, MINE, D), BF),
            pltpu.VMEM((3, MINE, D), BF),
            pltpu.VMEM((MINE, D), BF),
            pltpu.VMEM((8, MINE), F32),
            dma((3,)), dma((3,)),
            dma((4,)), dma((4,)),
            dma((4,)), dma((4,)),
            dma((3,)), dma((3,)),
            dma((7,)), dma((7,)),
            dma((7,)), dma((7,)),
            dma((3,)),
        ],
        compiler_params=pltpu.CompilerParams(
            collective_id=2, has_side_effects=True, vmem_limit_bytes=LIMIT
        ),
        name="mlp",
    )(n, stream, up, down, head_w, head_b)


def body(
    tokens, cross_qkv, cross_out, depth_qkv, depth_out, up_proj, down_proj, gains, head_weight, head_bias
):
    gz = lax.axis_index("gz")
    enc = table()
    dep2 = jnp.asarray(np.repeat(enc[:DP], 2, 0))
    enc = jnp.asarray(enc)

    def pad(a, rows):
        return jnp.pad(a, ((0, rows - a.shape[0]), (0, 0)))

    shard = jnp.concatenate(
        [pad(cross_qkv.T, 40), pad(cross_out, 16), pad(depth_qkv.T, 40), pad(depth_out, 16)]
    )
    shard = jnp.stack([shard[:, :HALF], shard[:, HALF:]])
    by_line = jnp.transpose(tokens, (0, 2, 1, 3)).reshape(LINES, XLD, D)
    by_column = tokens.reshape(GZ, 2, DPD, D)
    by_column = jnp.transpose(by_column, (0, 2, 1, 3)).reshape(GZ, 2 * DPD, D)
    lines, cols, w = gather(shard, by_line, by_column)
    mixed = line_attention(lines.reshape(XL, D), enc, gains[0:1], w)
    mixed = back(mixed.reshape(GX, 2, D))
    stream, n = column_attention(
        mixed.reshape(MINE, D), cols.reshape(MINE, D), enc, dep2, gains, w
    )
    feat, time = mlp(n, stream, up_proj, down_proj, head_weight[None], head_bias[None])
    feat = jnp.transpose(feat.reshape(INL, 2, DPD, 2, D), (0, 1, 3, 2, 4))
    feat = feat.reshape(INL, XLD, DPD, D)
    time = lax.dynamic_slice_in_dim(time[:, 0, :], 16 * gz, 16, 1)
    time = jnp.transpose(time.reshape(INL, 2, DPD, 2), (0, 1, 3, 2)).reshape(INL, XLD, DPD)
    return feat, time


def solution(mesh):
    return jax.shard_map(
        body,
        mesh=mesh,
        in_specs=(
            P(None, "gx", "gz", None),
            P(None, "gx"),
            P("gx", None),
            P(None, "gx"),
            P("gx", None),
            P(None, "gz"),
            P("gz", None),
            P(),
            P(),
            P(),
        ),
        out_specs=(P(None, "gx", "gz", None), P(None, "gx", "gz")),
        check_vma=False,
    )
```

```python
import functools
import math

import jax
import jax.numpy as jnp
import numpy as np
from jax import lax
from jax.experimental import pallas as pl
from jax.experimental.pallas import tpu as pltpu
from jax.sharding import PartitionSpec as P

ZN, YN, XN = 16, 4, 4
GX, GZ = ZN * YN, XN * 2
D, HEADS, HDIM, FF = 768, 12, 64, 3072
HALF = D // 2
INL, XL, DP = 4, 256, 64
XLD, DPD = XL // GX, DP // GZ
LINES = INL * DPD
MINE = 2 * DP
QKV_ROWS, OUT_ROWS = 144, 48
KIND = QKV_ROWS + OUT_ROWS
BLOCK = 2 * KIND
QKV, SPAN = 3 * D, 4 * D
PIECE = 48
SLOT = 112
MESH = pl.DeviceIdType.MESH
BF, F32 = jnp.bfloat16, jnp.float32
ANY = pl.BlockSpec(memory_space=pl.ANY)
VM = pl.BlockSpec(memory_space=pltpu.VMEM)
LIMIT = 56 << 20


def table():
    k = np.arange(D // 2)
    freq = math.pi * np.exp(-math.log(256.0) * k / (D // 2))
    angle = np.arange(XL)[:, None] * freq[None, :]
    return np.stack([np.sin(angle), np.cos(angle)], -1).reshape(XL, D).astype(np.float32)


def packing():
    one = np.zeros((BLOCK, YN * SLOT), np.float32)
    row = 0
    for at, count in ((0, 36), (40, 12), (56, 36), (96, 12)):
        for y in range(YN):
            for r in range(count):
                one[row, y * SLOT + at + r] = 1
                row += 1
    return one


def place():
    gx, gz = lax.axis_index("gx"), lax.axis_index("gz")
    return gx, gz, gx // YN, gx % YN, gz // 2, gz % 2


def rcopy(src, dst, send, recv, gx, gz):
    return pltpu.make_async_remote_copy(
        src_ref=src, dst_ref=dst, send_sem=send, recv_sem=recv, device_id=(gx, gz), device_id_type=MESH
    )


def signal(gx, gz):
    pl.semaphore_signal(
        pltpu.get_barrier_semaphore(), inc=1, device_id=(gx, gz), device_id_type=MESH
    )


def nt(a, b):
    return lax.dot_general(a, b, (((1,), (1,)), ((), ())), preferred_element_type=F32)


def normed(stream, gain):
    scale = lax.rsqrt(jnp.mean(stream * stream, -1, keepdims=True) + 1e-05)
    return (stream * scale * gain).astype(BF)


def which_axis(shape):
    return (lax.broadcasted_iota(jnp.int32, shape, 1) // 2) % 3


def rows16(start, size):
    return pl.ds(pl.multiple_of(start, 16), size)


def block_kernel(
    tok, w1, w2, w3, w4, gains, head_w, head_b, one_ref, enc_h, dep2_h, up_h, down_h,
    feat, time,
    enc, dep2, up, down, sbuf, shard, ybuf, block, w, by_line, lines, cols, nbuf,
    kbuf, qbuf, vbuf, obuf, sendb, mixed, nown, tokens, sent, pair, sums, got, stage, fbuf, gbuf, frecv, trecv,
    y_s, y_r, t_s, t_r, c_s, c_r, z_s, z_r, p_s, p_r, b_s, b_r, i_s, i_r, k_s, k_r,
    g_s, g_r, a_s, a_r, q_s, q_r, s_s, s_r, f_s, f_r, h_s, h_r, l_s,
):
    gx, gz, z, y, x, c = place()
    half = gx // 32
    own_line = half == c
    sib = 2 * x + 1 - c
    inl = (gx % 32) // 8
    dep = DPD * (2 * x + half) + gx % 8
    me_too = inl == x

    def greet_lines(i, _):
        there = 32 * c + i

        @pl.when(jnp.logical_or(there != gx, half != c))
        def _():
            signal(there, 2 * x + half)

        return 0

    lax.fori_loop(0, 32, greet_lines, 0)

    def greet_back(i, _):
        there, other = 32 * ((i // 8) % 2) + 8 * x + i % 8, 2 * (i // 16) + c

        @pl.when(jnp.logical_or(there != gx, other != gz))
        def _():
            signal(there, other)

        return 0

    lax.fori_loop(0, 64, greet_back, 0)
    for d in range(1, 4):
        signal(z * YN + (y + d) % YN, gz)
    signal(((z + 1) % ZN) * YN + y, gz)
    signal(((z + 15) % ZN) * YN + y, gz)
    for d in range(1, 8):
        signal(gx, (gz + d) % GZ)

    loads = [
        pltpu.make_async_copy(a, b, l_s.at[k])
        for k, (a, b) in enumerate(((enc_h, enc), (dep2_h, dep2), (up_h, up), (down_h, down)))
    ]
    for load in loads:
        load.start()
    sbuf[...] = jnp.zeros_like(sbuf)
    sbuf[0:36, :] = w1[...].astype(F32).T
    sbuf[40:52, :] = w2[...].astype(F32)
    sbuf[56:92, :] = w3[...].astype(F32).T
    sbuf[96:108, :] = w4[...].astype(F32)
    shard[0] = sbuf[:, :HALF].astype(BF)
    shard[1] = sbuf[:, HALF:].astype(BF)
    by_line[...] = (
        jnp.transpose(tok[...].astype(F32), (0, 2, 1, 3)).reshape(LINES, XLD, D).astype(BF)
    )
    pl.semaphore_wait(
        pltpu.get_barrier_semaphore(),
        12 + 32 + 64 - jnp.where(own_line, 1, 0) - jnp.where(me_too, 1, 0),
    )

    def y_copy(d):
        return rcopy(
            shard.at[c], ybuf.at[y], y_s.at[d - 1], y_r.at[d - 1], z * YN + (y + d) % YN, gz
        )

    own_y = pltpu.make_async_copy(shard.at[c], ybuf.at[y], l_s.at[4])
    own_y.start()
    for d in (1, 3, 2):
        y_copy(d).start()

    def t_copy(i):
        return rcopy(by_line.at[i], lines.at[gx], t_s.at[i], t_r, 32 * c + i, 2 * x + half)

    def t_start(i, _):
        here = jnp.logical_and(32 * c + i == gx, own_line)

        @pl.when(jnp.logical_not(here))
        def _():
            t_copy(i).start()

        @pl.when(here)
        def _():
            pltpu.make_async_copy(by_line.at[i], lines.at[gx], t_r).start()

        return 0

    lax.fori_loop(0, 32, t_start, 0)

    def c_copy(d):
        there = (gz + d) % GZ
        return rcopy(
            tok.at[there // 2, pl.ds(2 * (there % 2), 2)], cols.at[gz], c_s.at[d - 1], c_r.at[d - 1], gx, there
        )

    own_c = pltpu.make_async_copy(tok.at[x, pl.ds(2 * c, 2)], cols.at[gz], l_s.at[5])
    own_c.start()
    for d in range(1, 8):
        c_copy(d).start()

    own_y.wait()
    for d in range(1, 4):
        y_copy(d).wait_recv()
    block[...] = jnp.dot(
        one_ref[...], ybuf[...].reshape(YN * SLOT, HALF), preferred_element_type=F32
    ).astype(BF)

    def who(kind):
        return x if kind else y

    def near(kind, d):
        if kind:
            return gx, ((x + d) % XN) * 2 + c
        return z * YN + (y + d) % YN, gz

    def piece(kind, zsrc, k):
        at = SPAN * kind + jnp.where(k < 3, QKV_ROWS * zsrc + PIECE * k, QKV + PIECE * zsrc)
        return w.at[c, rows16(at, PIECE)]

    def parts(kind, zsrc, core):
        return (
            w.at[core, rows16(SPAN * kind + QKV_ROWS * zsrc, QKV_ROWS)],
            w.at[core, rows16(SPAN * kind + QKV + OUT_ROWS * zsrc, OUT_ROWS)],
        )

    own_parts = [
        pltpu.make_async_copy(
            block.at[pl.ds(KIND * kind + (0, QKV_ROWS)[k], (QKV_ROWS, OUT_ROWS)[k])],
            parts(kind, z, c)[k],
            l_s.at[6 + 2 * kind + k],
        )
        for kind in range(2)
        for k in range(2)
    ]
    for cp in own_parts:
        cp.start()

    def ring(kind, way, s, first=False):
        back = s - 1
        zsrc = (z + (ZN - back if way == 0 else back)) % ZN
        znext = (z + (1 if way == 0 else ZN - 1)) % ZN
        to = piece(kind, zsrc, who(kind))
        src = block.at[rows16(KIND * kind + PIECE * who(kind), PIECE)] if first else to
        return rcopy(
            src, to, z_s.at[kind, way, s - 1], z_r.at[kind, way, s - 1], znext * YN + y, gz
        )

    def arrived(kind, way, s):
        zsrc = (z + (ZN - s if way == 0 else s)) % ZN
        here = piece(kind, zsrc, who(kind))
        rcopy(here, here, z_s.at[kind, way, s - 1], z_r.at[kind, way, s - 1], gx, gz).wait_recv()
        return zsrc

    def spread(kind, zsrc):
        mine = piece(kind, zsrc, who(kind))
        return [
            rcopy(mine, mine, p_s.at[kind, zsrc, n], p_r.at[kind, zsrc, n], *near(kind, d))
            for n, d in enumerate((1, 3))
        ]

    def onward(kind, zsrc):
        odd = zsrc % 2
        it = piece(kind, zsrc, (who(kind) + jnp.where(odd == 0, 3, 1)) % 4)
        return rcopy(
            it, it, p_s.at[kind, zsrc, 2], p_r.at[kind, zsrc, 2], *near(kind, jnp.where(odd == 0, 1, 3))
        )

    def relay(kind, zsrc):
        return [
            rcopy(a, a, b_s.at[kind, zsrc, k], b_r.at[kind, zsrc, k], gx, sib)
            for k, a in enumerate(parts(kind, zsrc, c))
        ]

    def collect_near(kind, zsrc):
        for n, d in enumerate((3, 1)):
            here = piece(kind, zsrc, (who(kind) + d) % 4)
            rcopy(here, here, p_s.at[kind, zsrc, n], p_r.at[kind, zsrc, n], gx, gz).wait_recv()
        onward(kind, zsrc).start()

    def collect_far(kind, zsrc):
        here = piece(kind, zsrc, (who(kind) + 2) % 4)
        rcopy(here, here, p_s.at[kind, zsrc, 2], p_r.at[kind, zsrc, 2], gx, gz).wait_recv()
        for cp in relay(kind, zsrc):
            cp.start()

    def begin(kind):
        for way in range(2):
            ring(kind, way, 1, True).start()
        for cp in own_parts[2 * kind : 2 * kind + 2]:
            cp.wait()
        for cp in relay(kind, z):
            cp.start()

    def step(kind, s):
        @pl.when(s <= 8)
        def _():
            zsrc = arrived(kind, 0, s)

            @pl.when(s < 8)
            def _():
                ring(kind, 0, s + 1).start()

            for cp in spread(kind, zsrc):
                cp.start()

        @pl.when(s <= 7)
        def _():
            zsrc = arrived(kind, 1, s)

            @pl.when(s < 7)
            def _():
                ring(kind, 1, s + 1).start()

            for cp in spread(kind, zsrc):
                cp.start()

        @pl.when(jnp.logical_and(s >= 2, s <= 9))
        def _():
            collect_near(kind, (z + ZN - s + 1) % ZN)

        @pl.when(jnp.logical_and(s >= 2, s <= 8))
        def _():
            collect_near(kind, (z + s - 1) % ZN)

        @pl.when(jnp.logical_and(s >= 3, s <= 10))
        def _():
            collect_far(kind, (z + ZN - s + 2) % ZN)

        @pl.when(jnp.logical_and(s >= 3, s <= 9))
        def _():
            collect_far(kind, (z + s - 2) % ZN)

    def siblings(kind):
        def one(zsrc, _):
            for k, a in enumerate(parts(kind, zsrc, 1 - c)):
                rcopy(a, a, b_s.at[kind, zsrc, k], b_r.at[kind, zsrc, k], gx, gz).wait_recv()
            return 0

        lax.fori_loop(0, ZN, one, 0)

    def l_copy():
        mine = lines.at[rows16(32 * c, 32)]
        return rcopy(mine, mine, i_s, i_r, gx, sib)

    begin(0)

    def cross_step(s, _):
        step(0, s)

        @pl.when(s == 6)
        def _():
            mine = lines.at[rows16(32 * c, 32)]
            pltpu.make_async_copy(mine, mine, t_r).wait()
            l_copy().start()

        return 0

    lax.fori_loop(1, 9, cross_step, 0)
    begin(1)
    lax.fori_loop(9, 11, cross_step, 0)

    loads[0].wait()
    loads[1].wait()
    theirs = lines.at[rows16(32 * (1 - c), 32)]
    rcopy(theirs, theirs, i_s, i_r, gx, gz).wait_recv()
    which = which_axis((XL, D))
    pos = jnp.where(
        which == 1, enc[...], jnp.where(which == 0, enc[pl.ds(inl, 1), :], enc[pl.ds(dep, 1), :])
    )
    nbuf[...] = normed(lines[...].astype(F32).reshape(XL, D) + pos, gains[0:1, :])
    q = lax.broadcasted_iota(jnp.int32, (MINE, XL), 0)
    r = lax.broadcasted_iota(jnp.int32, (MINE, XL), 1)
    pick = jnp.where(r == 4 * (q // 2) + 2 * c + q % 2, 1.0, 0.0).astype(BF)
    nown[...] = jnp.dot(pick, nbuf[...], preferred_element_type=F32).astype(BF)

    def attend(base, keys_in, queries_in, count, mask, between):
        def project(part, tokens_in, left):
            a, b = (w[k, base + part * D : base + (part + 1) * D, :] for k in range(2))
            lo, hi = tokens_in[:, :HALF], tokens_in[:, HALF:]
            return (nt(a, lo) + nt(b, hi) if left else nt(lo, a) + nt(hi, b)).astype(BF)

        qbuf[...] = project(0, queries_in, True)
        kbuf[0:count, :] = project(1, keys_in, False)
        vbuf[:, 0:count] = project(2, keys_in, True)

        def two(p, _):
            keys = kbuf[0:count, pl.ds(pl.multiple_of(128 * p, 128), 128)]
            for j in range(2):
                at = rows16(128 * p + HDIM * j, HDIM)
                scores = jnp.dot(
                    keys[:, HDIM * j : HDIM * (j + 1)], qbuf[at, :], preferred_element_type=F32
                ) * (HDIM**-0.5)
                if mask is not None:
                    scores = jnp.where(mask, scores, -1e30)
                expo = jnp.exp(scores - jnp.max(scores, 0, keepdims=True))
                total = jnp.sum(expo, 0, keepdims=True)
                obuf[at, :] = (
                    jnp.dot(vbuf[at, 0:count], expo.astype(BF), preferred_element_type=F32) / total
                )
            if between:
                between(p)
            return 0

        lax.fori_loop(0, HEADS // 2, two, 0)

    siblings(0)
    attend(0, nbuf, nown, XL, None, lambda p: step(1, p + 1))
    sendb[...] = obuf[...].T.reshape(GX, 2, D).astype(BF)

    def k_copy(i):
        return rcopy(sendb.at[i], mixed.at[dep], k_s.at[i], k_r, i, 2 * inl + c)

    def k_start(i, _):
        here = jnp.logical_and(i == gx, me_too)

        @pl.when(jnp.logical_not(here))
        def _():
            k_copy(i).start()

        @pl.when(here)
        def _():
            pltpu.make_async_copy(sendb.at[i], mixed.at[dep], k_r).start()

        return 0

    lax.fori_loop(0, 64, k_start, 0)

    def depth_step(s, _):
        step(1, s)
        return 0

    lax.fori_loop(7, 11, depth_step, 0)

    own_c.wait()
    for d in range(1, 8):
        c_copy(d).wait_recv()
    which = which_axis((MINE, D))
    odd = lax.broadcasted_iota(jnp.int32, (MINE, D), 0) % 2
    first = XLD * gx + 2 * c
    cross = jnp.where(odd == 0, enc[pl.ds(first, 1), :], enc[pl.ds(first + 1, 1), :])
    pos = jnp.where(which == 1, cross, jnp.where(which == 0, enc[pl.ds(x, 1), :], dep2[...]))
    stream = jnp.transpose(cols[...].astype(F32), (0, 2, 1, 3)).reshape(MINE, D) + pos

    def project_out(v, base):
        return jnp.concatenate(
            [
                jnp.dot(v, w[k, base : base + D, :], preferred_element_type=F32)
                for k in range(2)
            ],
            1,
        )

    pltpu.make_async_copy(mixed, mixed, k_r).wait()
    stream = stream + project_out(mixed[...].reshape(MINE, D), QKV)
    nown[...] = normed(stream, gains[1:2, :])
    mask = (
        lax.broadcasted_iota(jnp.int32, (MINE, MINE), 0)
        + lax.broadcasted_iota(jnp.int32, (MINE, MINE), 1)
    ) % 2 == 0
    siblings(1)
    attend(SPAN, nown, nown, MINE, mask, None)
    stream = stream + project_out(obuf[...].T.astype(BF), SPAN + QKV)
    nown[...] = normed(stream, gains[2:3, :])

    def chip(d):
        return ((x + d) % XN) * 2 + c

    def to_near(d):
        n = 0 if d == 1 else 1
        return rcopy(nown, tokens.at[d, c], g_s.at[n], g_r.at[n], gx, chip(d))

    def to_far(n):
        rows = pl.ds(64 * n, 64)
        return rcopy(
            tokens.at[1 if n == 0 else 3, c, rows], tokens.at[2, c, rows],
            g_s.at[2 + n], g_r.at[2 + n], gx, chip(1 if n == 0 else 3),
        )

    def to_sib(d):
        src = nown if d == 0 else tokens.at[d, c]
        return rcopy(src, tokens.at[d, c], a_s.at[d], a_r.at[d], gx, sib)

    def from_sib(d):
        here = tokens.at[d, 1 - c]
        return rcopy(here, here, a_s.at[d], a_r.at[d], gx, sib)

    def pair_copy(d):
        return rcopy(sent.at[d, 1 - c], pair.at[d], q_s.at[d], q_r.at[d], gx, sib)

    def home(d):
        n = 0 if d == 1 else 1
        return rcopy(sums.at[d], got.at[d], s_s.at[n], s_r.at[n], gx, chip(4 - d))

    def home_far(n, hop):
        rows = pl.ds(64 * n, 64)
        src, dst = (sums.at[2, rows], stage.at[n]) if hop == 0 else (stage.at[n], got.at[2, rows])
        k = 2 + 2 * hop + n
        return rcopy(src, dst, s_s.at[k], s_r.at[k], gx, chip(1 if n == 0 else 3))

    to_near(1).start()
    to_near(3).start()
    to_sib(0).start()
    own_n = pltpu.make_async_copy(nown, tokens.at[0, c], l_s.at[10])
    own_n.start()
    loads[2].wait()
    loads[3].wait()

    def hidden_part(d):
        rows = tokens[d].reshape(2 * MINE, D)
        hidden = jax.nn.gelu(jnp.dot(rows, up[...], preferred_element_type=F32)).astype(BF)
        part = jnp.dot(hidden, down[...], preferred_element_type=F32).astype(BF)
        sent[d] = part.reshape(2, MINE, D)
        pair_copy(d).start()

    def both(d):
        pair_copy(d).wait_recv()
        return sent[d, c].astype(F32) + pair[d].astype(F32)

    own_n.wait()
    from_sib(0).wait_recv()
    hidden_part(0)
    for n, d in ((0, 1), (1, 3)):
        to_near(d).wait_recv()
        to_far(n).start()
        to_sib(d).start()
    from_sib(1).wait_recv()
    hidden_part(1)
    for n in range(2):
        to_far(n).wait_recv()
    to_sib(2).start()
    from_sib(3).wait_recv()
    hidden_part(3)
    sums[1] = both(1).astype(BF)
    home(1).start()
    from_sib(2).wait_recv()
    hidden_part(2)
    sums[3] = both(3).astype(BF)
    home(3).start()
    sums[2] = both(2).astype(BF)
    for n in range(2):
        home_far(n, 0).start()
    stream = stream + both(0)
    for n in range(2):
        home_far(n, 0).wait_recv()
        home_far(n, 1).start()
    for d in (1, 3):
        home(d).wait_recv()
        stream = stream + got[d].astype(F32)
    for n in range(2):
        home_far(n, 1).wait_recv()
    stream = stream + got[2].astype(F32)

    fbuf[...] = stream.astype(BF)

    def f_copy(d):
        there = (gz + d) % GZ
        return rcopy(fbuf.at[rows16(16 * there, 16)], frecv.at[gz], f_s.at[d - 1], f_r.at[d - 1], gx, there)

    own_f = pltpu.make_async_copy(fbuf.at[rows16(16 * gz, 16)], frecv.at[gz], l_s.at[11])
    own_f.start()
    for d in range(1, 8):
        f_copy(d).start()
    thick = jax.nn.softplus(jnp.sum(stream * head_w[...], -1, keepdims=True) + head_b[0, 0])
    i = lax.broadcasted_iota(jnp.int32, (MINE, MINE), 0)
    j = lax.broadcasted_iota(jnp.int32, (MINE, MINE), 1)
    across = jnp.broadcast_to(thick, (MINE, MINE)).T
    keep = jnp.logical_and(j <= i, (i + j) % 2 == 0)
    line = jnp.sum(jnp.where(keep, across, 0.0), 1, keepdims=True)
    gbuf[...] = jnp.broadcast_to(line, (MINE, 128))

    def h_copy(d):
        there = (gz + d) % GZ
        return rcopy(gbuf.at[rows16(16 * there, 16)], trecv.at[gz], h_s.at[d - 1], h_r.at[d - 1], gx, there)

    own_h = pltpu.make_async_copy(gbuf.at[rows16(16 * gz, 16)], trecv.at[gz], l_s.at[12])
    own_h.start()
    for d in range(1, 8):
        h_copy(d).start()
    own_f.wait()
    for d in range(1, 8):
        f_copy(d).wait_recv()
    feat[...] = (
        jnp.transpose(frecv[...].astype(F32).reshape(GZ, DPD, 2, D), (0, 2, 1, 3))
        .reshape(INL, XLD, DPD, D)
        .astype(BF)
    )
    own_h.wait()
    for d in range(1, 8):
        h_copy(d).wait_recv()
    row = lax.broadcasted_iota(jnp.int32, (GZ, 16, 128), 1)
    lane = lax.broadcasted_iota(jnp.int32, (GZ, 16, 128), 2)
    for k in range(2):
        mark = jnp.logical_and(row // 2 == lane, row % 2 == k)
        picked = jnp.sum(jnp.where(mark, trecv[...], 0.0), 1)
        for n in range(GZ):
            time[n // 2, 2 * (n % 2) + k : 2 * (n % 2) + k + 1, :] = picked[n : n + 1, :DPD]

    for d in range(1, 4):
        y_copy(d).wait_send()
    for d in range(1, 8):
        c_copy(d).wait_send()
        f_copy(d).wait_send()
        h_copy(d).wait_send()

    def t_end(i, _):
        @pl.when(jnp.logical_not(jnp.logical_and(32 * c + i == gx, own_line)))
        def _():
            t_copy(i).wait_send()

        return 0

    lax.fori_loop(0, 32, t_end, 0)

    def k_end(i, _):
        @pl.when(jnp.logical_not(jnp.logical_and(i == gx, me_too)))
        def _():
            k_copy(i).wait_send()

        return 0

    lax.fori_loop(0, 64, k_end, 0)
    l_copy().wait_send()
    for kind in range(2):
        for way in range(2):
            ring(kind, way, 1, True).wait_send()

        def r_end(s, _):
            ring(kind, 0, s).wait_send()

            @pl.when(s < 8)
            def _():
                ring(kind, 1, s).wait_send()

            return 0

        lax.fori_loop(2, 9, r_end, 0)

        def w_end(k, _):
            zsrc = (z + k) % ZN

            @pl.when(k > 0)
            def _():
                for cp in spread(kind, zsrc):
                    cp.wait_send()
                onward(kind, zsrc).wait_send()

            for cp in relay(kind, zsrc):
                cp.wait_send()
            return 0

        lax.fori_loop(0, ZN, w_end, 0)
    for d in (1, 3):
        to_near(d).wait_send()
        home(d).wait_send()
    for n in range(2):
        to_far(n).wait_send()
        home_far(n, 0).wait_send()
        home_far(n, 1).wait_send()
    for d in range(4):
        to_sib(d).wait_send()
        pair_copy(d).wait_send()


def body(
    tokens, cross_qkv, cross_out, depth_qkv, depth_out, up_proj, down_proj, gains, head_weight, head_bias
):
    enc = table()
    dep2 = jnp.asarray(np.repeat(enc[:DP], 2, 0))
    enc = jnp.asarray(enc)
    dma = pltpu.SemaphoreType.DMA
    vmem = pltpu.VMEM
    return pl.pallas_call(
        block_kernel,
        out_shape=(
            jax.ShapeDtypeStruct((INL, XLD, DPD, D), BF),
            jax.ShapeDtypeStruct((INL, XLD, DPD), F32),
        ),
        in_specs=[VM] * 7 + [pl.BlockSpec(memory_space=pltpu.SMEM), VM] + [ANY] * 4,
        out_specs=(VM, VM),
        scratch_shapes=[
            vmem((XL, D), F32),
            vmem((MINE, D), F32),
            vmem((D, FF // GZ), BF),
            vmem((FF // GZ, D), BF),
            vmem((SLOT, D), F32),
            vmem((2, SLOT, HALF), BF),
            vmem((YN, SLOT, HALF), BF),
            vmem((BLOCK, HALF), BF),
            vmem((2, 2 * SPAN, HALF), BF),
            vmem((LINES, XLD, D), BF),
            vmem((GX, XLD, D), BF),
            vmem((GZ, 2, DPD, D), BF),
            vmem((XL, D), BF),
            vmem((XL, D), BF),
            vmem((D, MINE), BF),
            vmem((D, XL), BF),
            vmem((D, MINE), F32),
            vmem((GX, 2, D), BF),
            vmem((DP, 2, D), BF),
            vmem((MINE, D), BF),
            vmem((4, 2, MINE, D), BF),
            vmem((4, 2, MINE, D), BF),
            vmem((4, MINE, D), BF),
            vmem((4, MINE, D), BF),
            vmem((4, MINE, D), BF),
            vmem((2, 64, D), BF),
            vmem((MINE, D), BF),
            vmem((MINE, 128), F32),
            vmem((GZ, 16, D), BF),
            vmem((GZ, 16, 128), F32),
            dma((3,)), dma((3,)),
            dma((32,)), dma,
            dma((7,)), dma((7,)),
            dma((2, 2, 8)), dma((2, 2, 8)),
            dma((2, ZN, 3)), dma((2, ZN, 3)),
            dma((2, ZN, 2)), dma((2, ZN, 2)),
            dma, dma,
            dma((64,)), dma,
            dma((4,)), dma((4,)),
            dma((4,)), dma((4,)),
            dma((4,)), dma((4,)),
            dma((6,)), dma((6,)),
            dma((7,)), dma((7,)),
            dma((7,)), dma((7,)),
            dma((13,)),
        ],
        compiler_params=pltpu.CompilerParams(
            collective_id=0, has_side_effects=True, vmem_limit_bytes=LIMIT
        ),
        name="axial_block",
    )(
        tokens, cross_qkv, cross_out, depth_qkv, depth_out, gains, head_weight[None], head_bias[None],
        jnp.asarray(packing(), BF), enc, dep2, up_proj, down_proj,
    )


def solution(mesh):
    return jax.shard_map(
        body,
        mesh=mesh,
        in_specs=(
            P(None, "gx", "gz", None),
            P(None, "gx"),
            P("gx", None),
            P(None, "gx"),
            P("gx", None),
            P(None, "gz"),
            P("gz", None),
            P(),
            P(),
            P(),
        ),
        out_specs=(P(None, "gx", "gz", None), P(None, "gx", "gz")),
        check_vma=False,
    )
```

```python
import functools
import math

import jax
import jax.numpy as jnp
import numpy as np
from jax import lax
from jax.experimental import pallas as pl
from jax.experimental.pallas import tpu as pltpu
from jax.sharding import PartitionSpec as P

ZN, YN, XN = 16, 4, 4
GX, GZ = ZN * YN, XN * 2
D, HEADS, HDIM, FF = 768, 12, 64, 3072
HALF = D // 2
INL, XL, DP = 4, 256, 64
XLD, DPD = XL // GX, DP // GZ
LINES = INL * DPD
MINE = 2 * DP
QKV_ROWS, OUT_ROWS = 144, 48
KIND = QKV_ROWS + OUT_ROWS
BLOCK = 2 * KIND
QKV, SPAN = 3 * D, 4 * D
PIECE, SUB = 48, 16
SLOT = 48
MESH = pl.DeviceIdType.MESH
BF, F32 = jnp.bfloat16, jnp.float32
ANY = pl.BlockSpec(memory_space=pl.ANY)
VM = pl.BlockSpec(memory_space=pltpu.VMEM)
LIMIT = 56 << 20


def table():
    k = np.arange(D // 2)
    freq = math.pi * np.exp(-math.log(256.0) * k / (D // 2))
    angle = np.arange(XL)[:, None] * freq[None, :]
    return np.stack([np.sin(angle), np.cos(angle)], -1).reshape(XL, D).astype(np.float32)


def packing():
    one = np.zeros((KIND, YN * SLOT), np.float32)
    row = 0
    for at, count in ((0, 36), (36, 12)):
        for y in range(YN):
            for r in range(count):
                one[row, y * SLOT + at + r] = 1
                row += 1
    return one


def place():
    gx, gz = lax.axis_index("gx"), lax.axis_index("gz")
    return gx, gz, gx // YN, gx % YN, gz // 2, gz % 2


def rcopy(src, dst, send, recv, gx, gz):
    return pltpu.make_async_remote_copy(
        src_ref=src, dst_ref=dst, send_sem=send, recv_sem=recv, device_id=(gx, gz), device_id_type=MESH
    )


def signal(gx, gz):
    pl.semaphore_signal(
        pltpu.get_barrier_semaphore(), inc=1, device_id=(gx, gz), device_id_type=MESH
    )


def nt(a, b):
    return lax.dot_general(a, b, (((1,), (1,)), ((), ())), preferred_element_type=F32)


def normed(stream, gain):
    scale = lax.rsqrt(jnp.mean(stream * stream, -1, keepdims=True) + 1e-05)
    return (stream * scale * gain).astype(BF)


def which_axis(shape):
    return (lax.broadcasted_iota(jnp.int32, shape, 1) // 2) % 3


def rows16(start, size):
    return pl.ds(pl.multiple_of(start, 16), size)


def block_kernel(
    tok, w1, w2, w3, w4, gains, head_w, head_b, one_ref, enc_h, dep2_h, up_h, down_h,
    feat, time,
    enc, dep2, up, down, sbuf, shard, mine_y, ybuf, block, w, by_line, lines, cols, nbuf,
    kbuf, qbuf, vbuf, obuf, sendb, mixed, nown, pairtok, acc, sent, pair, fbuf, gbuf, frecv, trecv,
    y_s, y_r, t_s, t_r, c_s, c_r, z_s, z_r, x_s, x_r, p_s, p_r, b_s, b_r, i_s, i_r, k_s, k_r,
    m_s, m_r, a_s, a_r, f_s, f_r, h_s, h_r, l_s,
):
    gx, gz, z, y, x, c = place()
    half = gx // 32
    own_line = half == c
    sib = 2 * x + 1 - c
    inl = (gx % 32) // 8
    dep = DPD * (2 * x + half) + gx % 8
    me_too = inl == x

    def greet_lines(i, _):
        there = 32 * c + i

        @pl.when(jnp.logical_or(there != gx, half != c))
        def _():
            signal(there, 2 * x + half)

        return 0

    lax.fori_loop(0, 32, greet_lines, 0)

    def greet_back(i, _):
        there, other = 32 * ((i // 8) % 2) + 8 * x + i % 8, 2 * (i // 16) + c

        @pl.when(jnp.logical_or(there != gx, other != gz))
        def _():
            signal(there, other)

        return 0

    lax.fori_loop(0, 64, greet_back, 0)
    for d in range(1, 4):
        signal(z * YN + (y + d) % YN, gz)
    for d in range(1, ZN):
        signal(((z + d) % ZN) * YN + y, gz)
    for d in range(1, 8):
        signal(gx, (gz + d) % GZ)

    loads = [
        pltpu.make_async_copy(a, b, l_s.at[k])
        for k, (a, b) in enumerate(((enc_h, enc), (dep2_h, dep2), (up_h, up.at[x]), (down_h, down.at[x])))
    ]
    for load in loads:
        load.start()
    for kind, (a, b) in enumerate(((w1, w2), (w3, w4))):
        sbuf[0:36, :] = a[...].astype(F32)
        sbuf[36:48, :] = b[...].astype(F32)
        shard[0, kind] = sbuf[:, :HALF].astype(BF)
        shard[1, kind] = sbuf[:, HALF:].astype(BF)
    by_line[...] = (
        jnp.transpose(tok[...].astype(F32), (0, 2, 1, 3)).reshape(LINES, XLD, D).astype(BF)
    )
    pl.semaphore_wait(
        pltpu.get_barrier_semaphore(),
        25 + 32 + 64 - jnp.where(own_line, 1, 0) - jnp.where(me_too, 1, 0),
    )

    def y_copy(kind, d):
        return rcopy(
            shard.at[c, kind], ybuf.at[kind, y], y_s.at[kind, d - 1], y_r.at[kind, d - 1],
            z * YN + (y + d) % YN, gz,
        )

    own_y = pltpu.make_async_copy(shard.at[c], mine_y, l_s.at[4])
    own_y.start()
    for d in (1, 3, 2):
        y_copy(0, d).start()

    def t_copy(i):
        return rcopy(by_line.at[i], lines.at[gx], t_s.at[i], t_r, 32 * c + i, 2 * x + half)

    def t_start(i, _):
        here = jnp.logical_and(32 * c + i == gx, own_line)

        @pl.when(jnp.logical_not(here))
        def _():
            t_copy(i).start()

        @pl.when(here)
        def _():
            pltpu.make_async_copy(by_line.at[i], lines.at[gx], t_r).start()

        return 0

    lax.fori_loop(0, 32, t_start, 0)

    def c_copy(d):
        there = (gz + d) % GZ
        return rcopy(
            tok.at[there // 2, pl.ds(2 * (there % 2), 2)], cols.at[gz], c_s.at[d - 1], c_r.at[d - 1], gx, there
        )

    own_c = pltpu.make_async_copy(tok.at[x, pl.ds(2 * c, 2)], cols.at[gz], l_s.at[5])
    own_c.start()
    for d in range(1, 8):
        c_copy(d).start()

    for d in (1, 3, 2):
        y_copy(1, d).start()
    own_y.wait()

    def pack(kind):
        for d in range(1, 4):
            y_copy(kind, d).wait_recv()
        for k in range(YN):

            @pl.when(k == y)
            def _():
                ybuf[kind, k] = mine_y[kind]

        block[KIND * kind : KIND * (kind + 1), :] = jnp.dot(
            one_ref[...], ybuf[kind].reshape(YN * SLOT, HALF), preferred_element_type=F32
        ).astype(BF)

    pack(0)

    def who(zsrc):
        return jnp.where(zsrc % 2 == 0, y, x)

    def seat(zsrc):
        return jnp.where(zsrc % 2 == 0, x, y)

    def near_x(d):
        return gx, ((x + d) % XN) * 2 + c

    def near(zsrc, d):
        even = zsrc % 2 == 0
        return (
            jnp.where(even, z * YN + (y + d) % YN, gx),
            jnp.where(even, gz, ((x + d) % XN) * 2 + c),
        )

    def piece(kind, zsrc, k):
        at = SPAN * kind + jnp.where(k < 3, QKV_ROWS * zsrc + PIECE * k, QKV + PIECE * zsrc)
        return w.at[c, rows16(at, PIECE)]

    def parts(kind, zsrc, core):
        return (
            w.at[core, rows16(SPAN * kind + QKV_ROWS * zsrc, QKV_ROWS)],
            w.at[core, rows16(SPAN * kind + QKV + OUT_ROWS * zsrc, OUT_ROWS)],
        )

    own_parts = [
        pltpu.make_async_copy(
            block.at[pl.ds(KIND * kind + (0, QKV_ROWS)[k], (QKV_ROWS, OUT_ROWS)[k])],
            parts(kind, z, c)[k],
            l_s.at[6 + 2 * kind + k],
        )
        for kind in range(2)
        for k in range(2)
    ]
    def sub(kind, zsrc, n):
        at = QKV_ROWS * zsrc + PIECE * who(zsrc) + SUB * n
        out = QKV + PIECE * zsrc + SUB * n
        return w.at[c, rows16(SPAN * kind + jnp.where(who(zsrc) < 3, at, out), SUB)]

    def z_copy(kind, d):
        at = KIND * kind + PIECE * who(z) + SUB * seat(z)
        return rcopy(
            block.at[rows16(at, SUB)], sub(kind, z, seat(z)),
            z_s.at[kind, d - 1], z_r.at[kind, d - 1], ((z + d) % ZN) * YN + y, gz,
        )

    def x_copy(kind, zsrc, d):
        mine = sub(kind, zsrc, seat(zsrc))
        return rcopy(
            mine, mine, x_s.at[kind, zsrc, d - 1], x_r.at[kind, zsrc, d - 1], *near(zsrc + 1, d)
        )

    def spread(kind, zsrc):
        mine = piece(kind, zsrc, who(zsrc))
        return [
            rcopy(mine, mine, p_s.at[kind, zsrc, n], p_r.at[kind, zsrc, n], *near(zsrc, d))
            for n, d in enumerate((1, 3))
        ]

    def onward(kind, zsrc):
        turn = (zsrc // 2) % 2
        it = piece(kind, zsrc, (who(zsrc) + jnp.where(turn == 0, 3, 1)) % 4)
        return rcopy(
            it, it, p_s.at[kind, zsrc, 2], p_r.at[kind, zsrc, 2], *near(zsrc, jnp.where(turn == 0, 1, 3))
        )

    def relay(kind, zsrc):
        return [
            rcopy(a, a, b_s.at[kind, zsrc, k], b_r.at[kind, zsrc, k], gx, sib)
            for k, a in enumerate(parts(kind, zsrc, c))
        ]

    def collect_near(kind, zsrc):
        for n, d in enumerate((3, 1)):
            here = piece(kind, zsrc, (who(zsrc) + d) % 4)
            rcopy(here, here, p_s.at[kind, zsrc, n], p_r.at[kind, zsrc, n], gx, gz).wait_recv()
        onward(kind, zsrc).start()

    def collect_far(kind, zsrc):
        here = piece(kind, zsrc, (who(zsrc) + 2) % 4)
        rcopy(here, here, p_s.at[kind, zsrc, 2], p_r.at[kind, zsrc, 2], gx, gz).wait_recv()
        for cp in relay(kind, zsrc):
            cp.start()

    def begin(kind):
        for cp in own_parts[2 * kind : 2 * kind + 2]:
            cp.start()

        @pl.when(seat(z) < 3)
        def _():
            for k in range(1, 9):
                z_copy(kind, k).start()
                if k < 8:
                    z_copy(kind, ZN - k).start()

        for cp in own_parts[2 * kind : 2 * kind + 2]:
            cp.wait()
        for cp in relay(kind, z):
            cp.start()

    def source(i):
        d = jnp.where(i % 2 == 0, i // 2 + 1, ZN - 1 - i // 2)
        return (z + ZN - d) % ZN, d

    def stage(lag, i, do):
        @pl.when(jnp.logical_and(i >= lag, i < ZN - 1 + lag))
        def _():
            do(*source(i - lag))

    def step(kind, i):
        def from_z(zsrc, d):
            @pl.when(seat(zsrc) < 3)
            def _():
                here = sub(kind, zsrc, seat(zsrc))
                rcopy(here, here, z_s.at[kind, d - 1], z_r.at[kind, d - 1], gx, gz).wait_recv()
                for k in (1, 3, 2):
                    x_copy(kind, zsrc, k).start()

        def whole(zsrc, _):
            for k in range(1, 4):
                n = (seat(zsrc) + 4 - k) % 4

                @pl.when(n < 3)
                def _():
                    here = sub(kind, zsrc, n)
                    rcopy(
                        here, here, x_s.at[kind, zsrc, k - 1], x_r.at[kind, zsrc, k - 1], gx, gz
                    ).wait_recv()

            for cp in spread(kind, zsrc):
                cp.start()

        stage(0, i, from_z)
        stage(3, i, whole)
        stage(6, i, lambda zsrc, _: collect_near(kind, zsrc))
        stage(9, i, lambda zsrc, _: collect_far(kind, zsrc))

    def siblings(kind):
        def one(zsrc, _):
            for k, a in enumerate(parts(kind, zsrc, 1 - c)):
                rcopy(a, a, b_s.at[kind, zsrc, k], b_r.at[kind, zsrc, k], gx, gz).wait_recv()
            return 0

        lax.fori_loop(0, ZN, one, 0)

    def l_copy():
        mine = lines.at[rows16(32 * c, 32)]
        return rcopy(mine, mine, i_s, i_r, gx, sib)

    begin(0)

    def ring4(near_of, me, own, item, part, at):
        def first(n):
            return rcopy(own, item(me), m_s.at[at, n], m_r.at[at, n], *near_of((1, 3)[n]))

        def second(n):
            src = part((me + (3, 1)[n]) % 4, n)
            return rcopy(src, src, m_s.at[at, 2 + n], m_r.at[at, 2 + n], *near_of((1, 3)[n]))

        return first, second

    def near_y(d):
        return z * YN + (y + d) % YN, gz

    up_rings = [
        ring4(
            near_x, x, up_h.at[pl.ds(HALF * k, HALF)],
            lambda chip, k=k: up.at[chip, pl.ds(HALF * k, HALF)],
            lambda chip, n, k=k: up.at[chip, pl.ds(HALF * k + HALF // 2 * n, HALF // 2)],
            k,
        )
        for k in range(2)
    ]

    def quarter(chip, n=None, q=None):
        at = 96 * (y if q is None else q)
        return down.at[chip, rows16(at, 96) if n is None else rows16(at + 48 * n, 48)]

    down_ring = ring4(near_x, x, down_h.at[rows16(96 * y, 96)], quarter, quarter, 2)
    down_spread = []
    for d in (1, 3, 2):
        chip = (x + d) % XN
        down_spread.append(
            ring4(
                near_y, y, quarter(chip),
                lambda q, chip=chip: quarter(chip, None, q),
                lambda q, n, chip=chip: quarter(chip, n, q),
                2 + d,
            )
        )
    all_rings = [*up_rings, down_ring, *down_spread]

    def firsts(r):
        for n in range(2):
            r[0](n).start()

    def seconds(r):
        for n in range(2):
            r[0](n).wait_recv()
        for n in range(2):
            r[1](n).start()

    def finished(r):
        for n in range(2):
            r[1](n).wait_recv()

    firsts(down_ring)
    firsts(up_rings[0])

    def cross_step(i, _):
        step(0, i)

        @pl.when(i == 8)
        def _():
            pack(1)
            begin(1)

        @pl.when(i == 10)
        def _():
            mine = lines.at[rows16(32 * c, 32)]
            pltpu.make_async_copy(mine, mine, t_r).wait()
            l_copy().start()

        @pl.when(i >= 18)
        def _():
            step(1, i - 18)

        return 0

    lax.fori_loop(0, 24, cross_step, 0)

    loads[0].wait()
    loads[1].wait()
    theirs = lines.at[rows16(32 * (1 - c), 32)]
    rcopy(theirs, theirs, i_s, i_r, gx, gz).wait_recv()
    which = which_axis((XL, D))
    pos = jnp.where(
        which == 1, enc[...], jnp.where(which == 0, enc[pl.ds(inl, 1), :], enc[pl.ds(dep, 1), :])
    )
    nbuf[...] = normed(lines[...].astype(F32).reshape(XL, D) + pos, gains[0:1, :])
    q = lax.broadcasted_iota(jnp.int32, (MINE, XL), 0)
    r = lax.broadcasted_iota(jnp.int32, (MINE, XL), 1)
    pick = jnp.where(r == 4 * (q // 2) + 2 * c + q % 2, 1.0, 0.0).astype(BF)
    nown[...] = jnp.dot(pick, nbuf[...], preferred_element_type=F32).astype(BF)

    def attend(base, keys_in, queries_in, count, mask, between):
        def project(part, tokens_in, left):
            a, b = (w[k, base + part * D : base + (part + 1) * D, :] for k in range(2))
            lo, hi = tokens_in[:, :HALF], tokens_in[:, HALF:]
            return (nt(a, lo) + nt(b, hi) if left else nt(lo, a) + nt(hi, b)).astype(BF)

        qbuf[...] = project(0, queries_in, True)
        kbuf[0:count, :] = project(1, keys_in, False)
        vbuf[:, 0:count] = project(2, keys_in, True)

        def two(p, _):
            keys = kbuf[0:count, pl.ds(pl.multiple_of(128 * p, 128), 128)]
            for j in range(2):
                at = rows16(128 * p + HDIM * j, HDIM)
                scores = jnp.dot(
                    keys[:, HDIM * j : HDIM * (j + 1)], qbuf[at, :], preferred_element_type=F32
                ) * (HDIM**-0.5)
                if mask is not None:
                    scores = jnp.where(mask, scores, -1e30)
                expo = jnp.exp(scores - jnp.max(scores, 0, keepdims=True))
                total = jnp.sum(expo, 0, keepdims=True)
                obuf[at, :] = (
                    jnp.dot(vbuf[at, 0:count], expo.astype(BF), preferred_element_type=F32) / total
                )
            if between:
                between(p)
            return 0

        lax.fori_loop(0, HEADS // 2, two, 0)

    siblings(0)

    def depth_step(i, _):
        step(1, i)
        return 0

    attend(0, nbuf, nown, XL, None, lambda p: depth_step(6 + p, 0))
    sendb[...] = obuf[...].T.reshape(GX, 2, D).astype(BF)

    def k_copy(i):
        return rcopy(sendb.at[i], mixed.at[dep], k_s.at[i], k_r, i, 2 * inl + c)

    def k_start(i, _):
        here = jnp.logical_and(i == gx, me_too)

        @pl.when(jnp.logical_not(here))
        def _():
            k_copy(i).start()

        @pl.when(here)
        def _():
            pltpu.make_async_copy(sendb.at[i], mixed.at[dep], k_r).start()

        return 0

    lax.fori_loop(0, 64, k_start, 0)

    lax.fori_loop(12, 24, depth_step, 0)
    firsts(up_rings[1])
    seconds(down_ring)
    seconds(up_rings[0])
    firsts(down_spread[0])
    firsts(down_spread[1])

    own_c.wait()
    for d in range(1, 8):
        c_copy(d).wait_recv()
    which = which_axis((MINE, D))
    odd = lax.broadcasted_iota(jnp.int32, (MINE, D), 0) % 2
    first = XLD * gx + 2 * c
    cross = jnp.where(odd == 0, enc[pl.ds(first, 1), :], enc[pl.ds(first + 1, 1), :])
    pos = jnp.where(which == 1, cross, jnp.where(which == 0, enc[pl.ds(x, 1), :], dep2[...]))
    stream = jnp.transpose(cols[...].astype(F32), (0, 2, 1, 3)).reshape(MINE, D) + pos

    def project_out(v, base):
        return jnp.concatenate(
            [
                jnp.dot(v, w[k, base : base + D, :], preferred_element_type=F32)
                for k in range(2)
            ],
            1,
        )

    pltpu.make_async_copy(mixed, mixed, k_r).wait()
    stream = stream + project_out(mixed[...].reshape(MINE, D), QKV)
    nown[...] = normed(stream, gains[1:2, :])
    mask = (
        lax.broadcasted_iota(jnp.int32, (MINE, MINE), 0)
        + lax.broadcasted_iota(jnp.int32, (MINE, MINE), 1)
    ) % 2 == 0
    finished(down_ring)
    firsts(down_spread[2])
    siblings(1)
    seconds(down_spread[0])
    seconds(down_spread[1])
    seconds(up_rings[1])
    attend(SPAN, nown, nown, MINE, mask, None)
    stream = stream + project_out(obuf[...].T.astype(BF), SPAN + QKV)
    nown[...] = normed(stream, gains[2:3, :])

    def tok_copy():
        return rcopy(nown, pairtok.at[c], a_s.at[0], a_r.at[0], gx, sib)

    def sum_copy():
        return rcopy(sent, pair, a_s.at[1], a_r.at[1], gx, sib)

    seconds(down_spread[2])
    tok_copy().start()
    pairtok[c] = nown[...]
    loads[2].wait()
    loads[3].wait()
    there = pairtok.at[1 - c]
    rcopy(there, there, a_s.at[0], a_r.at[0], gx, gz).wait_recv()

    def hidden_part(k):
        both = pairtok[...].reshape(2 * MINE, D)
        hidden = jax.nn.gelu(jnp.dot(both, up[k], preferred_element_type=F32)).astype(BF)
        return jnp.dot(hidden, down[k], preferred_element_type=F32)

    for r in (*up_rings, *down_spread):
        finished(r)
    acc[...] = hidden_part(0) + hidden_part(1) + hidden_part(2) + hidden_part(3)
    sent[...] = acc[pl.ds(pl.multiple_of(MINE * (1 - c), MINE), MINE), :].astype(BF)
    sum_copy().start()
    stream = stream + acc[pl.ds(pl.multiple_of(MINE * c, MINE), MINE), :]
    sum_copy().wait_recv()
    stream = stream + pair[...].astype(F32)

    fbuf[...] = stream.astype(BF)

    def f_copy(d):
        there = (gz + d) % GZ
        return rcopy(fbuf.at[rows16(16 * there, 16)], frecv.at[gz], f_s.at[d - 1], f_r.at[d - 1], gx, there)

    own_f = pltpu.make_async_copy(fbuf.at[rows16(16 * gz, 16)], frecv.at[gz], l_s.at[11])
    own_f.start()
    for d in range(1, 8):
        f_copy(d).start()
    thick = jax.nn.softplus(jnp.sum(stream * head_w[...].reshape(1, D), -1, keepdims=True) + head_b[0])
    i = lax.broadcasted_iota(jnp.int32, (MINE, MINE), 0)
    j = lax.broadcasted_iota(jnp.int32, (MINE, MINE), 1)
    across = jnp.broadcast_to(thick, (MINE, MINE)).T
    keep = jnp.logical_and(j <= i, (i + j) % 2 == 0)
    line = jnp.sum(jnp.where(keep, across, 0.0), 1, keepdims=True)
    gbuf[...] = jnp.broadcast_to(line, (MINE, 128))

    def h_copy(d):
        there = (gz + d) % GZ
        return rcopy(gbuf.at[rows16(16 * there, 16)], trecv.at[gz], h_s.at[d - 1], h_r.at[d - 1], gx, there)

    own_h = pltpu.make_async_copy(gbuf.at[rows16(16 * gz, 16)], trecv.at[gz], l_s.at[12])
    own_h.start()
    for d in range(1, 8):
        h_copy(d).start()
    own_f.wait()
    for d in range(1, 8):
        f_copy(d).wait_recv()
    feat[...] = (
        jnp.transpose(frecv[...].astype(F32).reshape(GZ, DPD, 2, D), (0, 2, 1, 3))
        .reshape(INL, XLD, DPD, D)
        .astype(BF)
    )
    own_h.wait()
    for d in range(1, 8):
        h_copy(d).wait_recv()
    row = lax.broadcasted_iota(jnp.int32, (GZ, 16, 128), 1)
    lane = lax.broadcasted_iota(jnp.int32, (GZ, 16, 128), 2)
    for k in range(2):
        mark = jnp.logical_and(row // 2 == lane, row % 2 == k)
        picked = jnp.sum(jnp.where(mark, trecv[...], 0.0), 1)
        for n in range(GZ):
            time[n // 2, 2 * (n % 2) + k : 2 * (n % 2) + k + 1, :] = picked[n : n + 1, :DPD]

    for d in range(1, 4):
        y_copy(0, d).wait_send()
        y_copy(1, d).wait_send()
    for d in range(1, 8):
        c_copy(d).wait_send()
        f_copy(d).wait_send()
        h_copy(d).wait_send()

    def t_end(i, _):
        @pl.when(jnp.logical_not(jnp.logical_and(32 * c + i == gx, own_line)))
        def _():
            t_copy(i).wait_send()

        return 0

    lax.fori_loop(0, 32, t_end, 0)

    def k_end(i, _):
        @pl.when(jnp.logical_not(jnp.logical_and(i == gx, me_too)))
        def _():
            k_copy(i).wait_send()

        return 0

    lax.fori_loop(0, 64, k_end, 0)
    l_copy().wait_send()
    for kind in range(2):
        @pl.when(seat(z) < 3)
        def _():
            for d in range(1, ZN):
                z_copy(kind, d).wait_send()

        def w_end(k, _):
            zsrc = (z + k) % ZN

            @pl.when(k > 0)
            def _():
                @pl.when(seat(zsrc) < 3)
                def _():
                    for d in range(1, 4):
                        x_copy(kind, zsrc, d).wait_send()

                for cp in spread(kind, zsrc):
                    cp.wait_send()
                onward(kind, zsrc).wait_send()

            for cp in relay(kind, zsrc):
                cp.wait_send()
            return 0

        lax.fori_loop(0, ZN, w_end, 0)
    for r in all_rings:
        for n in range(2):
            r[0](n).wait_send()
            r[1](n).wait_send()
    tok_copy().wait_send()
    sum_copy().wait_send()


def body(
    tokens, cross_qkv, cross_out, depth_qkv, depth_out, up_proj, down_proj, gains, head_weight, head_bias
):
    enc = table()
    dep2 = jnp.asarray(np.repeat(enc[:DP], 2, 0))
    enc = jnp.asarray(enc)
    dma = pltpu.SemaphoreType.DMA
    vmem = pltpu.VMEM
    return pl.pallas_call(
        block_kernel,
        out_shape=(
            jax.ShapeDtypeStruct((INL, XLD, DPD, D), BF),
            jax.ShapeDtypeStruct((INL, XLD, DPD), F32),
        ),
        in_specs=[VM] * 7 + [pl.BlockSpec(memory_space=pltpu.SMEM), VM] + [ANY] * 4,
        out_specs=(VM, VM),
        scratch_shapes=[
            vmem((XL, D), F32),
            vmem((MINE, D), F32),
            vmem((XN, D, FF // GZ), BF),
            vmem((XN, FF // GZ, D), BF),
            vmem((SLOT, D), F32),
            vmem((2, 2, SLOT, HALF), BF),
            vmem((2, SLOT, HALF), BF),
            vmem((2, YN, SLOT, HALF), BF),
            vmem((BLOCK, HALF), BF),
            vmem((2, 2 * SPAN, HALF), BF),
            vmem((LINES, XLD, D), BF),
            vmem((GX, XLD, D), BF),
            vmem((GZ, 2, DPD, D), BF),
            vmem((XL, D), BF),
            vmem((XL, D), BF),
            vmem((D, MINE), BF),
            vmem((D, XL), BF),
            vmem((D, MINE), F32),
            vmem((GX, 2, D), BF),
            vmem((DP, 2, D), BF),
            vmem((MINE, D), BF),
            vmem((2, MINE, D), BF),
            vmem((2 * MINE, D), F32),
            vmem((MINE, D), BF),
            vmem((MINE, D), BF),
            vmem((MINE, D), BF),
            vmem((MINE, 128), F32),
            vmem((GZ, 16, D), BF),
            vmem((GZ, 16, 128), F32),
            dma((2, 3)), dma((2, 3)),
            dma((32,)), dma,
            dma((7,)), dma((7,)),
            dma((2, 15)), dma((2, 15)),
            dma((2, ZN, 3)), dma((2, ZN, 3)),
            dma((2, ZN, 3)), dma((2, ZN, 3)),
            dma((2, ZN, 2)), dma((2, ZN, 2)),
            dma, dma,
            dma((64,)), dma,
            dma((6, 4)), dma((6, 4)),
            dma((2,)), dma((2,)),
            dma((7,)), dma((7,)),
            dma((7,)), dma((7,)),
            dma((13,)),
        ],
        compiler_params=pltpu.CompilerParams(
            collective_id=0, has_side_effects=True, vmem_limit_bytes=LIMIT
        ),
        name="axial_block",
    )(
        tokens, cross_qkv.T, cross_out, depth_qkv.T, depth_out, gains, head_weight, head_bias,
        jnp.asarray(packing(), BF), enc, dep2, up_proj, down_proj,
    )


def solution(mesh):
    return jax.shard_map(
        body,
        mesh=mesh,
        in_specs=(
            P(None, "gx", "gz", None),
            P(None, "gx"),
            P("gx", None),
            P(None, "gx"),
            P("gx", None),
            P(None, "gz"),
            P("gz", None),
            P(),
            P(),
            P(),
        ),
        out_specs=(P(None, "gx", "gz", None), P(None, "gx", "gz")),
        check_vma=False,
    )
```

```python
import functools
import math

import jax
import jax.numpy as jnp
import numpy as np
from jax import lax
from jax.experimental import pallas as pl
from jax.experimental.pallas import tpu as pltpu
from jax.sharding import PartitionSpec as P

ZN, YN, XN = 16, 4, 4
GX, GZ = ZN * YN, XN * 2
D, HEADS, HDIM, FF = 768, 12, 64, 3072
HALF = D // 2
INL, XL, DP = 4, 256, 64
XLD, DPD = XL // GX, DP // GZ
LINES = INL * DPD
MINE = 2 * DP
QKV_ROWS, OUT_ROWS = 144, 48
KIND = QKV_ROWS + OUT_ROWS
BLOCK = 2 * KIND
QKV, SPAN = 3 * D, 4 * D
PIECE, SUB = 48, 16
LAG = 8
STEPS = ZN - 1 + 3 * LAG
SLOT = 48
MESH = pl.DeviceIdType.MESH
BF, F32 = jnp.bfloat16, jnp.float32
ANY = pl.BlockSpec(memory_space=pl.ANY)
VM = pl.BlockSpec(memory_space=pltpu.VMEM)
LIMIT = 56 << 20


def table():
    k = np.arange(D // 2)
    freq = math.pi * np.exp(-math.log(256.0) * k / (D // 2))
    angle = np.arange(XL)[:, None] * freq[None, :]
    return np.stack([np.sin(angle), np.cos(angle)], -1).reshape(XL, D).astype(np.float32)


def packing():
    one = np.zeros((KIND, YN * SLOT), np.float32)
    row = 0
    for at, count in ((0, 36), (36, 12)):
        for y in range(YN):
            for r in range(count):
                one[row, y * SLOT + at + r] = 1
                row += 1
    return one


def place():
    gx, gz = lax.axis_index("gx"), lax.axis_index("gz")
    return gx, gz, gx // YN, gx % YN, gz // 2, gz % 2


def rcopy(src, dst, send, recv, gx, gz):
    return pltpu.make_async_remote_copy(
        src_ref=src, dst_ref=dst, send_sem=send, recv_sem=recv, device_id=(gx, gz), device_id_type=MESH
    )


def signal(gx, gz):
    pl.semaphore_signal(
        pltpu.get_barrier_semaphore(), inc=1, device_id=(gx, gz), device_id_type=MESH
    )


def nt(a, b):
    return lax.dot_general(a, b, (((1,), (1,)), ((), ())), preferred_element_type=F32)


def normed(stream, gain):
    scale = lax.rsqrt(jnp.mean(stream * stream, -1, keepdims=True) + 1e-05)
    return (stream * scale * gain).astype(BF)


def which_axis(shape):
    return (lax.broadcasted_iota(jnp.int32, shape, 1) // 2) % 3


def rows16(start, size):
    return pl.ds(pl.multiple_of(start, 16), size)


def block_kernel(
    tok, w1, w2, w3, w4, gains, head_w, head_b, one_ref, enc_h, dep2_h, up_h, down_h,
    feat, time,
    enc, dep2, up, down, sbuf, shard, mine_y, ybuf, block, w, by_line, lines, cols, nbuf,
    kbuf, qbuf, vbuf, obuf, sendb, mixed, nown, pairtok, acc, sent, pair, fbuf, gbuf, frecv, trecv,
    y_s, y_r, t_s, t_r, c_s, c_r, z_s, z_r, x_s, x_r, p_s, p_r, b_s, b_r, i_s, i_r, k_s, k_r,
    m_s, m_r, a_s, a_r, f_s, f_r, h_s, h_r, l_s,
):
    gx, gz, z, y, x, c = place()
    half = gx // 32
    own_line = half == c
    sib = 2 * x + 1 - c
    inl = (gx % 32) // 8
    dep = DPD * (2 * x + half) + gx % 8
    me_too = inl == x

    def greet_lines(i, _):
        there = 32 * c + i

        @pl.when(jnp.logical_or(there != gx, half != c))
        def _():
            signal(there, 2 * x + half)

        return 0

    lax.fori_loop(0, 32, greet_lines, 0)

    def greet_back(i, _):
        there, other = 32 * ((i // 8) % 2) + 8 * x + i % 8, 2 * (i // 16) + c

        @pl.when(jnp.logical_or(there != gx, other != gz))
        def _():
            signal(there, other)

        return 0

    lax.fori_loop(0, 64, greet_back, 0)
    for d in range(1, 4):
        signal(z * YN + (y + d) % YN, gz)
    for d in range(1, ZN):
        signal(((z + d) % ZN) * YN + y, gz)
    for d in range(1, 8):
        signal(gx, (gz + d) % GZ)

    loads = [
        pltpu.make_async_copy(a, b, l_s.at[k])
        for k, (a, b) in enumerate(((enc_h, enc), (dep2_h, dep2), (up_h, up.at[x]), (down_h, down.at[x])))
    ]
    for load in loads:
        load.start()
    for kind, (a, b) in enumerate(((w1, w2), (w3, w4))):
        sbuf[0:36, :] = a[...].astype(F32)
        sbuf[36:48, :] = b[...].astype(F32)
        shard[0, kind] = sbuf[:, :HALF].astype(BF)
        shard[1, kind] = sbuf[:, HALF:].astype(BF)
    by_line[...] = (
        jnp.transpose(tok[...].astype(F32), (0, 2, 1, 3)).reshape(LINES, XLD, D).astype(BF)
    )
    pl.semaphore_wait(
        pltpu.get_barrier_semaphore(),
        25 + 32 + 64 - jnp.where(own_line, 1, 0) - jnp.where(me_too, 1, 0),
    )

    def y_copy(kind, d):
        return rcopy(
            shard.at[c, kind], ybuf.at[kind, y], y_s.at[kind, d - 1], y_r.at[kind, d - 1],
            z * YN + (y + d) % YN, gz,
        )

    own_y = pltpu.make_async_copy(shard.at[c], mine_y, l_s.at[4])
    own_y.start()
    for d in (1, 3, 2):
        y_copy(0, d).start()

    def t_copy(i):
        return rcopy(by_line.at[i], lines.at[gx], t_s.at[i], t_r, 32 * c + i, 2 * x + half)

    def t_start(i, _):
        here = jnp.logical_and(32 * c + i == gx, own_line)

        @pl.when(jnp.logical_not(here))
        def _():
            t_copy(i).start()

        @pl.when(here)
        def _():
            pltpu.make_async_copy(by_line.at[i], lines.at[gx], t_r).start()

        return 0

    lax.fori_loop(0, 32, t_start, 0)

    def c_copy(d):
        there = (gz + d) % GZ
        return rcopy(
            tok.at[there // 2, pl.ds(2 * (there % 2), 2)], cols.at[gz], c_s.at[d - 1], c_r.at[d - 1], gx, there
        )

    own_c = pltpu.make_async_copy(tok.at[x, pl.ds(2 * c, 2)], cols.at[gz], l_s.at[5])
    own_c.start()
    for d in range(1, 8):
        c_copy(d).start()

    for d in (1, 3, 2):
        y_copy(1, d).start()
    own_y.wait()

    def pack(kind):
        for d in range(1, 4):
            y_copy(kind, d).wait_recv()
        for k in range(YN):

            @pl.when(k == y)
            def _():
                ybuf[kind, k] = mine_y[kind]

        block[KIND * kind : KIND * (kind + 1), :] = jnp.dot(
            one_ref[...], ybuf[kind].reshape(YN * SLOT, HALF), preferred_element_type=F32
        ).astype(BF)

    pack(0)

    def who(zsrc):
        return jnp.where(zsrc % 2 == 0, y, x)

    def seat(zsrc):
        return jnp.where(zsrc % 2 == 0, x, y)

    def near_x(d):
        return gx, ((x + d) % XN) * 2 + c

    def near(zsrc, d):
        even = zsrc % 2 == 0
        return (
            jnp.where(even, z * YN + (y + d) % YN, gx),
            jnp.where(even, gz, ((x + d) % XN) * 2 + c),
        )

    def piece(kind, zsrc, k):
        at = SPAN * kind + jnp.where(k < 3, QKV_ROWS * zsrc + PIECE * k, QKV + PIECE * zsrc)
        return w.at[c, rows16(at, PIECE)]

    def parts(kind, zsrc, core):
        return (
            w.at[core, rows16(SPAN * kind + QKV_ROWS * zsrc, QKV_ROWS)],
            w.at[core, rows16(SPAN * kind + QKV + OUT_ROWS * zsrc, OUT_ROWS)],
        )

    own_parts = [
        pltpu.make_async_copy(
            block.at[pl.ds(KIND * kind + (0, QKV_ROWS)[k], (QKV_ROWS, OUT_ROWS)[k])],
            parts(kind, z, c)[k],
            l_s.at[6 + 2 * kind + k],
        )
        for kind in range(2)
        for k in range(2)
    ]
    def sub(kind, zsrc, n):
        at = QKV_ROWS * zsrc + PIECE * who(zsrc) + SUB * n
        out = QKV + PIECE * zsrc + SUB * n
        return w.at[c, rows16(SPAN * kind + jnp.where(who(zsrc) < 3, at, out), SUB)]

    def z_copy(kind, d):
        at = KIND * kind + PIECE * who(z) + SUB * seat(z)
        return rcopy(
            block.at[rows16(at, SUB)], sub(kind, z, seat(z)),
            z_s.at[kind, d - 1], z_r.at[kind, d - 1], ((z + d) % ZN) * YN + y, gz,
        )

    def x_copy(kind, zsrc, d):
        mine = sub(kind, zsrc, seat(zsrc))
        return rcopy(
            mine, mine, x_s.at[kind, zsrc, d - 1], x_r.at[kind, zsrc, d - 1], *near(zsrc + 1, d)
        )

    def spread(kind, zsrc):
        mine = piece(kind, zsrc, who(zsrc))
        return [
            rcopy(mine, mine, p_s.at[kind, zsrc, n], p_r.at[kind, zsrc, n], *near(zsrc, d))
            for n, d in enumerate((1, 3))
        ]

    def onward(kind, zsrc):
        turn = (zsrc // 2) % 2
        it = piece(kind, zsrc, (who(zsrc) + jnp.where(turn == 0, 3, 1)) % 4)
        return rcopy(
            it, it, p_s.at[kind, zsrc, 2], p_r.at[kind, zsrc, 2], *near(zsrc, jnp.where(turn == 0, 1, 3))
        )

    def relay(kind, zsrc):
        return [
            rcopy(a, a, b_s.at[kind, zsrc, k], b_r.at[kind, zsrc, k], gx, sib)
            for k, a in enumerate(parts(kind, zsrc, c))
        ]

    def collect_near(kind, zsrc):
        for n, d in enumerate((3, 1)):
            here = piece(kind, zsrc, (who(zsrc) + d) % 4)
            rcopy(here, here, p_s.at[kind, zsrc, n], p_r.at[kind, zsrc, n], gx, gz).wait_recv()
        onward(kind, zsrc).start()

    def collect_far(kind, zsrc):
        here = piece(kind, zsrc, (who(zsrc) + 2) % 4)
        rcopy(here, here, p_s.at[kind, zsrc, 2], p_r.at[kind, zsrc, 2], gx, gz).wait_recv()
        for cp in relay(kind, zsrc):
            cp.start()

    def begin(kind):
        for cp in own_parts[2 * kind : 2 * kind + 2]:
            cp.start()

        @pl.when(seat(z) < 3)
        def _():
            for k in range(1, 9):
                z_copy(kind, k).start()
                if k < 8:
                    z_copy(kind, ZN - k).start()

        for cp in own_parts[2 * kind : 2 * kind + 2]:
            cp.wait()
        for cp in relay(kind, z):
            cp.start()

    def source(i):
        d = jnp.where(i % 2 == 0, i // 2 + 1, ZN - 1 - i // 2)
        return (z + ZN - d) % ZN, d

    def stage(lag, i, do):
        @pl.when(jnp.logical_and(i >= lag, i < ZN - 1 + lag))
        def _():
            do(*source(i - lag))

    def step(kind, i):
        def from_z(zsrc, d):
            @pl.when(seat(zsrc) < 3)
            def _():
                here = sub(kind, zsrc, seat(zsrc))
                rcopy(here, here, z_s.at[kind, d - 1], z_r.at[kind, d - 1], gx, gz).wait_recv()
                for k in (1, 3, 2):
                    x_copy(kind, zsrc, k).start()

        def whole(zsrc, _):
            for k in range(1, 4):
                n = (seat(zsrc) + 4 - k) % 4

                @pl.when(n < 3)
                def _():
                    here = sub(kind, zsrc, n)
                    rcopy(
                        here, here, x_s.at[kind, zsrc, k - 1], x_r.at[kind, zsrc, k - 1], gx, gz
                    ).wait_recv()

            for cp in spread(kind, zsrc):
                cp.start()

        stage(0, i, from_z)
        stage(LAG, i, whole)
        stage(2 * LAG, i, lambda zsrc, _: collect_near(kind, zsrc))
        stage(3 * LAG, i, lambda zsrc, _: collect_far(kind, zsrc))

    def siblings(kind):
        def one(zsrc, _):
            for k, a in enumerate(parts(kind, zsrc, 1 - c)):
                rcopy(a, a, b_s.at[kind, zsrc, k], b_r.at[kind, zsrc, k], gx, gz).wait_recv()
            return 0

        lax.fori_loop(0, ZN, one, 0)

    def l_copy():
        mine = lines.at[rows16(32 * c, 32)]
        return rcopy(mine, mine, i_s, i_r, gx, sib)

    begin(0)

    def ring4(near_of, me, own, item, part, at):
        def first(n):
            return rcopy(own, item(me), m_s.at[at, n], m_r.at[at, n], *near_of((1, 3)[n]))

        def second(n):
            src = part((me + (3, 1)[n]) % 4, n)
            return rcopy(src, src, m_s.at[at, 2 + n], m_r.at[at, 2 + n], *near_of((1, 3)[n]))

        return first, second

    def near_y(d):
        return z * YN + (y + d) % YN, gz

    up_rings = [
        ring4(
            near_x, x, up_h.at[pl.ds(HALF * k, HALF)],
            lambda chip, k=k: up.at[chip, pl.ds(HALF * k, HALF)],
            lambda chip, n, k=k: up.at[chip, pl.ds(HALF * k + HALF // 2 * n, HALF // 2)],
            k,
        )
        for k in range(2)
    ]

    def quarter(chip, n=None, q=None):
        at = 96 * (y if q is None else q)
        return down.at[chip, rows16(at, 96) if n is None else rows16(at + 48 * n, 48)]

    down_ring = ring4(near_x, x, down_h.at[rows16(96 * y, 96)], quarter, quarter, 2)
    down_spread = []
    for d in (1, 3, 2):
        chip = (x + d) % XN
        down_spread.append(
            ring4(
                near_y, y, quarter(chip),
                lambda q, chip=chip: quarter(chip, None, q),
                lambda q, n, chip=chip: quarter(chip, n, q),
                2 + d,
            )
        )
    all_rings = [*up_rings, down_ring, *down_spread]

    def firsts(r):
        for n in range(2):
            r[0](n).start()

    def seconds(r):
        for n in range(2):
            r[0](n).wait_recv()
        for n in range(2):
            r[1](n).start()

    def finished(r):
        for n in range(2):
            r[1](n).wait_recv()

    firsts(down_ring)
    firsts(up_rings[0])

    def cross_step(i, _):
        step(0, i)

        @pl.when(i == 8)
        def _():
            pack(1)
            begin(1)

        @pl.when(i == 10)
        def _():
            mine = lines.at[rows16(32 * c, 32)]
            pltpu.make_async_copy(mine, mine, t_r).wait()
            l_copy().start()

        @pl.when(i >= STEPS - 15)
        def _():
            step(1, i - STEPS + 15)

        return 0

    lax.fori_loop(0, STEPS - 12, cross_step, 0)
    loads[0].wait()
    loads[1].wait()
    theirs = lines.at[rows16(32 * (1 - c), 32)]
    rcopy(theirs, theirs, i_s, i_r, gx, gz).wait_recv()
    which = which_axis((XL, D))
    pos = jnp.where(
        which == 1, enc[...], jnp.where(which == 0, enc[pl.ds(inl, 1), :], enc[pl.ds(dep, 1), :])
    )
    nbuf[...] = normed(lines[...].astype(F32).reshape(XL, D) + pos, gains[0:1, :])
    q = lax.broadcasted_iota(jnp.int32, (MINE, XL), 0)
    r = lax.broadcasted_iota(jnp.int32, (MINE, XL), 1)
    pick = jnp.where(r == 4 * (q // 2) + 2 * c + q % 2, 1.0, 0.0).astype(BF)
    nown[...] = jnp.dot(pick, nbuf[...], preferred_element_type=F32).astype(BF)

    lax.fori_loop(STEPS - 12, STEPS, cross_step, 0)

    def attend(base, keys_in, queries_in, count, mask, between):
        def project(part, tokens_in, left):
            a, b = (w[k, base + part * D : base + (part + 1) * D, :] for k in range(2))
            lo, hi = tokens_in[:, :HALF], tokens_in[:, HALF:]
            return (nt(a, lo) + nt(b, hi) if left else nt(lo, a) + nt(hi, b)).astype(BF)

        qbuf[...] = project(0, queries_in, True)
        kbuf[0:count, :] = project(1, keys_in, False)
        vbuf[:, 0:count] = project(2, keys_in, True)

        def two(p, _):
            keys = kbuf[0:count, pl.ds(pl.multiple_of(128 * p, 128), 128)]
            for j in range(2):
                at = rows16(128 * p + HDIM * j, HDIM)
                scores = jnp.dot(
                    keys[:, HDIM * j : HDIM * (j + 1)], qbuf[at, :], preferred_element_type=F32
                ) * (HDIM**-0.5)
                if mask is not None:
                    scores = jnp.where(mask, scores, -1e30)
                expo = jnp.exp(scores - jnp.max(scores, 0, keepdims=True))
                total = jnp.sum(expo, 0, keepdims=True)
                obuf[at, :] = (
                    jnp.dot(vbuf[at, 0:count], expo.astype(BF), preferred_element_type=F32) / total
                )
            if between:
                between(p)
            return 0

        lax.fori_loop(0, HEADS // 2, two, 0)

    siblings(0)

    def depth_step(i, _):
        step(1, i)
        return 0

    attend(0, nbuf, nown, XL, None, lambda p: lax.fori_loop(15 + 2 * p, 17 + 2 * p, depth_step, 0))
    sendb[...] = obuf[...].T.reshape(GX, 2, D).astype(BF)

    def k_copy(i):
        return rcopy(sendb.at[i], mixed.at[dep], k_s.at[i], k_r, i, 2 * inl + c)

    def k_start(i, _):
        here = jnp.logical_and(i == gx, me_too)

        @pl.when(jnp.logical_not(here))
        def _():
            k_copy(i).start()

        @pl.when(here)
        def _():
            pltpu.make_async_copy(sendb.at[i], mixed.at[dep], k_r).start()

        return 0

    lax.fori_loop(0, 64, k_start, 0)

    seconds(down_ring)
    seconds(up_rings[0])
    firsts(down_spread[0])
    firsts(down_spread[1])
    firsts(up_rings[1])
    lax.fori_loop(27, STEPS, depth_step, 0)

    finished(down_ring)
    firsts(down_spread[2])
    seconds(down_spread[0])
    seconds(down_spread[1])
    seconds(up_rings[1])

    own_c.wait()
    for d in range(1, 8):
        c_copy(d).wait_recv()
    which = which_axis((MINE, D))
    odd = lax.broadcasted_iota(jnp.int32, (MINE, D), 0) % 2
    first = XLD * gx + 2 * c
    cross = jnp.where(odd == 0, enc[pl.ds(first, 1), :], enc[pl.ds(first + 1, 1), :])
    pos = jnp.where(which == 1, cross, jnp.where(which == 0, enc[pl.ds(x, 1), :], dep2[...]))
    stream = jnp.transpose(cols[...].astype(F32), (0, 2, 1, 3)).reshape(MINE, D) + pos

    def project_out(v, base):
        return jnp.concatenate(
            [
                jnp.dot(v, w[k, base : base + D, :], preferred_element_type=F32)
                for k in range(2)
            ],
            1,
        )

    pltpu.make_async_copy(mixed, mixed, k_r).wait()
    stream = stream + project_out(mixed[...].reshape(MINE, D), QKV)
    nown[...] = normed(stream, gains[1:2, :])
    mask = (
        lax.broadcasted_iota(jnp.int32, (MINE, MINE), 0)
        + lax.broadcasted_iota(jnp.int32, (MINE, MINE), 1)
    ) % 2 == 0
    siblings(1)
    attend(SPAN, nown, nown, MINE, mask, None)
    stream = stream + project_out(obuf[...].T.astype(BF), SPAN + QKV)
    nown[...] = normed(stream, gains[2:3, :])

    def tok_copy():
        return rcopy(nown, pairtok.at[c], a_s.at[0], a_r.at[0], gx, sib)

    def sum_copy():
        return rcopy(sent, pair, a_s.at[1], a_r.at[1], gx, sib)

    seconds(down_spread[2])
    tok_copy().start()
    pairtok[c] = nown[...]
    loads[2].wait()
    loads[3].wait()
    there = pairtok.at[1 - c]
    rcopy(there, there, a_s.at[0], a_r.at[0], gx, gz).wait_recv()

    def hidden_part(k):
        both = pairtok[...].reshape(2 * MINE, D)
        hidden = jax.nn.gelu(jnp.dot(both, up[k], preferred_element_type=F32)).astype(BF)
        return jnp.dot(hidden, down[k], preferred_element_type=F32)

    for r in (*up_rings, *down_spread):
        finished(r)
    acc[...] = hidden_part(0) + hidden_part(1) + hidden_part(2) + hidden_part(3)
    sent[...] = acc[pl.ds(pl.multiple_of(MINE * (1 - c), MINE), MINE), :].astype(BF)
    sum_copy().start()
    stream = stream + acc[pl.ds(pl.multiple_of(MINE * c, MINE), MINE), :]
    sum_copy().wait_recv()
    stream = stream + pair[...].astype(F32)

    fbuf[...] = stream.astype(BF)

    def f_copy(d):
        there = (gz + d) % GZ
        return rcopy(fbuf.at[rows16(16 * there, 16)], frecv.at[gz], f_s.at[d - 1], f_r.at[d - 1], gx, there)

    own_f = pltpu.make_async_copy(fbuf.at[rows16(16 * gz, 16)], frecv.at[gz], l_s.at[11])
    own_f.start()
    for d in range(1, 8):
        f_copy(d).start()
    thick = jax.nn.softplus(jnp.sum(stream * head_w[...].reshape(1, D), -1, keepdims=True) + head_b[0])
    i = lax.broadcasted_iota(jnp.int32, (MINE, MINE), 0)
    j = lax.broadcasted_iota(jnp.int32, (MINE, MINE), 1)
    across = jnp.broadcast_to(thick, (MINE, MINE)).T
    keep = jnp.logical_and(j <= i, (i + j) % 2 == 0)
    line = jnp.sum(jnp.where(keep, across, 0.0), 1, keepdims=True)
    gbuf[...] = jnp.broadcast_to(line, (MINE, 128))

    def h_copy(d):
        there = (gz + d) % GZ
        return rcopy(gbuf.at[rows16(16 * there, 16)], trecv.at[gz], h_s.at[d - 1], h_r.at[d - 1], gx, there)

    own_h = pltpu.make_async_copy(gbuf.at[rows16(16 * gz, 16)], trecv.at[gz], l_s.at[12])
    own_h.start()
    for d in range(1, 8):
        h_copy(d).start()
    for d in range(1, 4):
        y_copy(0, d).wait_send()
        y_copy(1, d).wait_send()
    for d in range(1, 8):
        c_copy(d).wait_send()

    def t_end(i, _):
        @pl.when(jnp.logical_not(jnp.logical_and(32 * c + i == gx, own_line)))
        def _():
            t_copy(i).wait_send()

        return 0

    lax.fori_loop(0, 32, t_end, 0)

    def k_end(i, _):
        @pl.when(jnp.logical_not(jnp.logical_and(i == gx, me_too)))
        def _():
            k_copy(i).wait_send()

        return 0

    lax.fori_loop(0, 64, k_end, 0)
    l_copy().wait_send()
    for kind in range(2):
        @pl.when(seat(z) < 3)
        def _():
            for d in range(1, ZN):
                z_copy(kind, d).wait_send()

        def w_end(k, _):
            zsrc = (z + k) % ZN

            @pl.when(k > 0)
            def _():
                @pl.when(seat(zsrc) < 3)
                def _():
                    for d in range(1, 4):
                        x_copy(kind, zsrc, d).wait_send()

                for cp in spread(kind, zsrc):
                    cp.wait_send()
                onward(kind, zsrc).wait_send()

            for cp in relay(kind, zsrc):
                cp.wait_send()
            return 0

        lax.fori_loop(0, ZN, w_end, 0)
    for r in all_rings:
        for n in range(2):
            r[0](n).wait_send()
            r[1](n).wait_send()
    tok_copy().wait_send()
    sum_copy().wait_send()
    own_f.wait()
    for d in range(1, 8):
        f_copy(d).wait_recv()
    feat[...] = (
        jnp.transpose(frecv[...].astype(F32).reshape(GZ, DPD, 2, D), (0, 2, 1, 3))
        .reshape(INL, XLD, DPD, D)
        .astype(BF)
    )
    own_h.wait()
    for d in range(1, 8):
        h_copy(d).wait_recv()
    row = lax.broadcasted_iota(jnp.int32, (GZ, 16, 128), 1)
    lane = lax.broadcasted_iota(jnp.int32, (GZ, 16, 128), 2)
    for k in range(2):
        mark = jnp.logical_and(row // 2 == lane, row % 2 == k)
        picked = jnp.sum(jnp.where(mark, trecv[...], 0.0), 1)
        for n in range(GZ):
            time[n // 2, 2 * (n % 2) + k : 2 * (n % 2) + k + 1, :] = picked[n : n + 1, :DPD]
    for d in range(1, 8):
        f_copy(d).wait_send()
        h_copy(d).wait_send()


def body(
    tokens, cross_qkv, cross_out, depth_qkv, depth_out, up_proj, down_proj, gains, head_weight, head_bias
):
    enc = table()
    dep2 = jnp.asarray(np.repeat(enc[:DP], 2, 0))
    enc = jnp.asarray(enc)
    dma = pltpu.SemaphoreType.DMA
    vmem = pltpu.VMEM
    return pl.pallas_call(
        block_kernel,
        out_shape=(
            jax.ShapeDtypeStruct((INL, XLD, DPD, D), BF),
            jax.ShapeDtypeStruct((INL, XLD, DPD), F32),
        ),
        in_specs=[VM] * 7 + [pl.BlockSpec(memory_space=pltpu.SMEM), VM] + [ANY] * 4,
        out_specs=(VM, VM),
        scratch_shapes=[
            vmem((XL, D), F32),
            vmem((MINE, D), F32),
            vmem((XN, D, FF // GZ), BF),
            vmem((XN, FF // GZ, D), BF),
            vmem((SLOT, D), F32),
            vmem((2, 2, SLOT, HALF), BF),
            vmem((2, SLOT, HALF), BF),
            vmem((2, YN, SLOT, HALF), BF),
            vmem((BLOCK, HALF), BF),
            vmem((2, 2 * SPAN, HALF), BF),
            vmem((LINES, XLD, D), BF),
            vmem((GX, XLD, D), BF),
            vmem((GZ, 2, DPD, D), BF),
            vmem((XL, D), BF),
            vmem((XL, D), BF),
            vmem((D, MINE), BF),
            vmem((D, XL), BF),
            vmem((D, MINE), F32),
            vmem((GX, 2, D), BF),
            vmem((DP, 2, D), BF),
            vmem((MINE, D), BF),
            vmem((2, MINE, D), BF),
            vmem((2 * MINE, D), F32),
            vmem((MINE, D), BF),
            vmem((MINE, D), BF),
            vmem((MINE, D), BF),
            vmem((MINE, 128), F32),
            vmem((GZ, 16, D), BF),
            vmem((GZ, 16, 128), F32),
            dma((2, 3)), dma((2, 3)),
            dma((32,)), dma,
            dma((7,)), dma((7,)),
            dma((2, 15)), dma((2, 15)),
            dma((2, ZN, 3)), dma((2, ZN, 3)),
            dma((2, ZN, 3)), dma((2, ZN, 3)),
            dma((2, ZN, 2)), dma((2, ZN, 2)),
            dma, dma,
            dma((64,)), dma,
            dma((6, 4)), dma((6, 4)),
            dma((2,)), dma((2,)),
            dma((7,)), dma((7,)),
            dma((7,)), dma((7,)),
            dma((13,)),
        ],
        compiler_params=pltpu.CompilerParams(
            collective_id=0, has_side_effects=True, vmem_limit_bytes=LIMIT
        ),
        name="axial_block",
    )(
        tokens, cross_qkv.T, cross_out, depth_qkv.T, depth_out, gains, head_weight, head_bias,
        jnp.asarray(packing(), BF), enc, dep2, up_proj, down_proj,
    )


def solution(mesh):
    return jax.shard_map(
        body,
        mesh=mesh,
        in_specs=(
            P(None, "gx", "gz", None),
            P(None, "gx"),
            P("gx", None),
            P(None, "gx"),
            P("gx", None),
            P(None, "gz"),
            P("gz", None),
            P(),
            P(),
            P(),
        ),
        out_specs=(P(None, "gx", "gz", None), P(None, "gx", "gz")),
        check_vma=False,
    )
```

```python
import functools
import math

import jax
import jax.numpy as jnp
import numpy as np
from jax import lax
from jax.experimental import pallas as pl
from jax.experimental.pallas import tpu as pltpu
from jax.sharding import PartitionSpec as P

ZN, YN, XN = 16, 4, 4
GX, GZ = ZN * YN, XN * 2
D, HEADS, HDIM, FF = 768, 12, 64, 3072
HALF = D // 2
INL, XL, DP = 4, 256, 64
XLD, DPD = XL // GX, DP // GZ
LINES = INL * DPD
MINE = 2 * DP
QKV_ROWS, OUT_ROWS = 144, 48
KIND = QKV_ROWS + OUT_ROWS
BLOCK = 2 * KIND
QKV, SPAN = 3 * D, 4 * D
PIECE, SUB = 48, 16
LAG = 6
STEPS = ZN - 1 + 3 * LAG
SLOT = 48
MESH = pl.DeviceIdType.MESH
BF, F32 = jnp.bfloat16, jnp.float32
ANY = pl.BlockSpec(memory_space=pl.ANY)
VM = pl.BlockSpec(memory_space=pltpu.VMEM)
LIMIT = 56 << 20


def table():
    k = np.arange(D // 2)
    freq = math.pi * np.exp(-math.log(256.0) * k / (D // 2))
    angle = np.arange(XL)[:, None] * freq[None, :]
    return np.stack([np.sin(angle), np.cos(angle)], -1).reshape(XL, D).astype(np.float32)


def packing():
    one = np.zeros((KIND, YN * SLOT), np.float32)
    row = 0
    for at, count in ((0, 36), (36, 12)):
        for y in range(YN):
            for r in range(count):
                one[row, y * SLOT + at + r] = 1
                row += 1
    return one


def place():
    gx, gz = lax.axis_index("gx"), lax.axis_index("gz")
    return gx, gz, gx // YN, gx % YN, gz // 2, gz % 2


def rcopy(src, dst, send, recv, gx, gz):
    return pltpu.make_async_remote_copy(
        src_ref=src, dst_ref=dst, send_sem=send, recv_sem=recv, device_id=(gx, gz), device_id_type=MESH
    )


def signal(gx, gz):
    pl.semaphore_signal(
        pltpu.get_barrier_semaphore(), inc=1, device_id=(gx, gz), device_id_type=MESH
    )


def nt(a, b):
    return lax.dot_general(a, b, (((1,), (1,)), ((), ())), preferred_element_type=F32)


def normed(stream, gain):
    scale = lax.rsqrt(jnp.mean(stream * stream, -1, keepdims=True) + 1e-05)
    return (stream * scale * gain).astype(BF)


def which_axis(shape):
    return (lax.broadcasted_iota(jnp.int32, shape, 1) // 2) % 3


def rows16(start, size):
    return pl.ds(pl.multiple_of(start, 16), size)


def block_kernel(
    tok, w1, w2, w3, w4, gains, head_w, head_b, one_ref, enc_h, dep2_h, up_h, down_h,
    feat, time,
    enc, dep2, up, down, sbuf, shard, mine_y, ybuf, block, w, by_line, lines, cols, nbuf,
    kbuf, qbuf, vbuf, obuf, sendb, mixed, nown, pairtok, acc, sent, pair, fbuf, gbuf, frecv, trecv,
    y_s, y_r, t_s, t_r, c_s, c_r, z_s, z_r, x_s, x_r, p_s, p_r, b_s, b_r, i_s, i_r, k_s, k_r,
    m_s, m_r, a_s, a_r, f_s, f_r, h_s, h_r, l_s,
):
    gx, gz, z, y, x, c = place()
    half = gx // 32
    own_line = half == c
    sib = 2 * x + 1 - c
    inl = (gx % 32) // 8
    dep = DPD * (2 * x + half) + gx % 8
    me_too = inl == x

    def greet_lines(i, _):
        there = 32 * c + i

        @pl.when(jnp.logical_or(there != gx, half != c))
        def _():
            signal(there, 2 * x + half)

        return 0

    lax.fori_loop(0, 32, greet_lines, 0)

    def greet_back(i, _):
        there, other = 32 * ((i // 8) % 2) + 8 * x + i % 8, 2 * (i // 16) + c

        @pl.when(jnp.logical_or(there != gx, other != gz))
        def _():
            signal(there, other)

        return 0

    lax.fori_loop(0, 64, greet_back, 0)
    for d in range(1, 4):
        signal(z * YN + (y + d) % YN, gz)
    for d in range(1, ZN):
        signal(((z + d) % ZN) * YN + y, gz)
    for d in range(1, 8):
        signal(gx, (gz + d) % GZ)

    loads = [
        pltpu.make_async_copy(a, b, l_s.at[k])
        for k, (a, b) in enumerate(((enc_h, enc), (dep2_h, dep2), (up_h, up.at[x]), (down_h, down.at[x])))
    ]
    for load in loads:
        load.start()
    for kind, (a, b) in enumerate(((w1, w2), (w3, w4))):
        sbuf[0:36, :] = a[...].astype(F32)
        sbuf[36:48, :] = b[...].astype(F32)
        shard[0, kind] = sbuf[:, :HALF].astype(BF)
        shard[1, kind] = sbuf[:, HALF:].astype(BF)
    by_line[...] = (
        jnp.transpose(tok[...].astype(F32), (0, 2, 1, 3)).reshape(LINES, XLD, D).astype(BF)
    )
    pl.semaphore_wait(
        pltpu.get_barrier_semaphore(),
        25 + 32 + 64 - jnp.where(own_line, 1, 0) - jnp.where(me_too, 1, 0),
    )

    def y_copy(kind, d):
        return rcopy(
            shard.at[c, kind], ybuf.at[kind, y], y_s.at[kind, d - 1], y_r.at[kind, d - 1],
            z * YN + (y + d) % YN, gz,
        )

    own_y = pltpu.make_async_copy(shard.at[c], mine_y, l_s.at[4])
    own_y.start()
    for d in (1, 3, 2):
        y_copy(0, d).start()

    def t_copy(i):
        return rcopy(by_line.at[i], lines.at[gx], t_s.at[i], t_r, 32 * c + i, 2 * x + half)

    def t_start(i, _):
        here = jnp.logical_and(32 * c + i == gx, own_line)

        @pl.when(jnp.logical_not(here))
        def _():
            t_copy(i).start()

        @pl.when(here)
        def _():
            pltpu.make_async_copy(by_line.at[i], lines.at[gx], t_r).start()

        return 0

    lax.fori_loop(0, 32, t_start, 0)

    def c_copy(d):
        there = (gz + d) % GZ
        return rcopy(
            tok.at[there // 2, pl.ds(2 * (there % 2), 2)], cols.at[gz], c_s.at[d - 1], c_r.at[d - 1], gx, there
        )

    own_c = pltpu.make_async_copy(tok.at[x, pl.ds(2 * c, 2)], cols.at[gz], l_s.at[5])
    own_c.start()
    for d in range(1, 8):
        c_copy(d).start()

    for d in (1, 3, 2):
        y_copy(1, d).start()
    own_y.wait()

    def pack(kind):
        for d in range(1, 4):
            y_copy(kind, d).wait_recv()
        for k in range(YN):

            @pl.when(k == y)
            def _():
                ybuf[kind, k] = mine_y[kind]

        block[KIND * kind : KIND * (kind + 1), :] = jnp.dot(
            one_ref[...], ybuf[kind].reshape(YN * SLOT, HALF), preferred_element_type=F32
        ).astype(BF)

    pack(0)

    def who(zsrc):
        return jnp.where(zsrc % 2 == 0, y, x)

    def seat(zsrc):
        return jnp.where(zsrc % 2 == 0, x, y)

    def near_x(d):
        return gx, ((x + d) % XN) * 2 + c

    def near(zsrc, d):
        even = zsrc % 2 == 0
        return (
            jnp.where(even, z * YN + (y + d) % YN, gx),
            jnp.where(even, gz, ((x + d) % XN) * 2 + c),
        )

    def piece(kind, zsrc, k):
        at = SPAN * kind + jnp.where(k < 3, QKV_ROWS * zsrc + PIECE * k, QKV + PIECE * zsrc)
        return w.at[c, rows16(at, PIECE)]

    def parts(kind, zsrc, core):
        return (
            w.at[core, rows16(SPAN * kind + QKV_ROWS * zsrc, QKV_ROWS)],
            w.at[core, rows16(SPAN * kind + QKV + OUT_ROWS * zsrc, OUT_ROWS)],
        )

    own_parts = [
        pltpu.make_async_copy(
            block.at[pl.ds(KIND * kind + (0, QKV_ROWS)[k], (QKV_ROWS, OUT_ROWS)[k])],
            parts(kind, z, c)[k],
            l_s.at[6 + 2 * kind + k],
        )
        for kind in range(2)
        for k in range(2)
    ]
    def sub(kind, zsrc, n):
        at = QKV_ROWS * zsrc + PIECE * who(zsrc) + SUB * n
        out = QKV + PIECE * zsrc + SUB * n
        return w.at[c, rows16(SPAN * kind + jnp.where(who(zsrc) < 3, at, out), SUB)]

    def z_copy(kind, d):
        at = KIND * kind + PIECE * who(z) + SUB * seat(z)
        return rcopy(
            block.at[rows16(at, SUB)], sub(kind, z, seat(z)),
            z_s.at[kind, d - 1], z_r.at[kind, d - 1], ((z + d) % ZN) * YN + y, gz,
        )

    def x_copy(kind, zsrc, d):
        mine = sub(kind, zsrc, seat(zsrc))
        return rcopy(
            mine, mine, x_s.at[kind, zsrc, d - 1], x_r.at[kind, zsrc, d - 1], *near(zsrc + 1, d)
        )

    def spread(kind, zsrc):
        mine = piece(kind, zsrc, who(zsrc))
        return [
            rcopy(mine, mine, p_s.at[kind, zsrc, n], p_r.at[kind, zsrc, n], *near(zsrc, d))
            for n, d in enumerate((1, 3))
        ]

    def onward(kind, zsrc):
        turn = (zsrc // 2) % 2
        it = piece(kind, zsrc, (who(zsrc) + jnp.where(turn == 0, 3, 1)) % 4)
        return rcopy(
            it, it, p_s.at[kind, zsrc, 2], p_r.at[kind, zsrc, 2], *near(zsrc, jnp.where(turn == 0, 1, 3))
        )

    def relay(kind, zsrc):
        return [
            rcopy(a, a, b_s.at[kind, zsrc, k], b_r.at[kind, zsrc, k], gx, sib)
            for k, a in enumerate(parts(kind, zsrc, c))
        ]

    def collect_near(kind, zsrc):
        for n, d in enumerate((3, 1)):
            here = piece(kind, zsrc, (who(zsrc) + d) % 4)
            rcopy(here, here, p_s.at[kind, zsrc, n], p_r.at[kind, zsrc, n], gx, gz).wait_recv()
        onward(kind, zsrc).start()

    def collect_far(kind, zsrc):
        here = piece(kind, zsrc, (who(zsrc) + 2) % 4)
        rcopy(here, here, p_s.at[kind, zsrc, 2], p_r.at[kind, zsrc, 2], gx, gz).wait_recv()
        for cp in relay(kind, zsrc):
            cp.start()

    def begin(kind):
        for cp in own_parts[2 * kind : 2 * kind + 2]:
            cp.start()

        @pl.when(seat(z) < 3)
        def _():
            for k in range(1, 9):
                z_copy(kind, k).start()
                if k < 8:
                    z_copy(kind, ZN - k).start()

        for cp in own_parts[2 * kind : 2 * kind + 2]:
            cp.wait()
        for cp in relay(kind, z):
            cp.start()

    def source(i):
        d = jnp.where(i % 2 == 0, i // 2 + 1, ZN - 1 - i // 2)
        return (z + ZN - d) % ZN, d

    def stage(lag, i, do):
        @pl.when(jnp.logical_and(i >= lag, i < ZN - 1 + lag))
        def _():
            do(*source(i - lag))

    def step(kind, i):
        def from_z(zsrc, d):
            @pl.when(seat(zsrc) < 3)
            def _():
                here = sub(kind, zsrc, seat(zsrc))
                rcopy(here, here, z_s.at[kind, d - 1], z_r.at[kind, d - 1], gx, gz).wait_recv()
                for k in (1, 3, 2):
                    x_copy(kind, zsrc, k).start()

        def whole(zsrc, _):
            for k in range(1, 4):
                n = (seat(zsrc) + 4 - k) % 4

                @pl.when(n < 3)
                def _():
                    here = sub(kind, zsrc, n)
                    rcopy(
                        here, here, x_s.at[kind, zsrc, k - 1], x_r.at[kind, zsrc, k - 1], gx, gz
                    ).wait_recv()

            for cp in spread(kind, zsrc):
                cp.start()

        stage(0, i, from_z)
        stage(LAG, i, whole)
        stage(2 * LAG, i, lambda zsrc, _: collect_near(kind, zsrc))
        stage(3 * LAG, i, lambda zsrc, _: collect_far(kind, zsrc))

    def siblings(kind):
        def one(zsrc, _):
            for k, a in enumerate(parts(kind, zsrc, 1 - c)):
                rcopy(a, a, b_s.at[kind, zsrc, k], b_r.at[kind, zsrc, k], gx, gz).wait_recv()
            return 0

        lax.fori_loop(0, ZN, one, 0)

    def l_copy():
        mine = lines.at[rows16(32 * c, 32)]
        return rcopy(mine, mine, i_s, i_r, gx, sib)

    begin(0)

    def ring4(near_of, me, own, item, part, at):
        def first(n):
            return rcopy(own, item(me), m_s.at[at, n], m_r.at[at, n], *near_of((1, 3)[n]))

        def second(n):
            src = part((me + (3, 1)[n]) % 4, n)
            return rcopy(src, src, m_s.at[at, 2 + n], m_r.at[at, 2 + n], *near_of((1, 3)[n]))

        return first, second

    def near_y(d):
        return z * YN + (y + d) % YN, gz

    up_rings = [
        ring4(
            near_x, x, up_h.at[pl.ds(HALF * k, HALF)],
            lambda chip, k=k: up.at[chip, pl.ds(HALF * k, HALF)],
            lambda chip, n, k=k: up.at[chip, pl.ds(HALF * k + HALF // 2 * n, HALF // 2)],
            k,
        )
        for k in range(2)
    ]

    def quarter(chip, n=None, q=None):
        at = 96 * (y if q is None else q)
        return down.at[chip, rows16(at, 96) if n is None else rows16(at + 48 * n, 48)]

    down_ring = ring4(near_x, x, down_h.at[rows16(96 * y, 96)], quarter, quarter, 2)
    down_spread = []
    for d in (1, 3, 2):
        chip = (x + d) % XN
        down_spread.append(
            ring4(
                near_y, y, quarter(chip),
                lambda q, chip=chip: quarter(chip, None, q),
                lambda q, n, chip=chip: quarter(chip, n, q),
                2 + d,
            )
        )
    all_rings = [*up_rings, down_ring, *down_spread]

    def firsts(r):
        for n in range(2):
            r[0](n).start()

    def seconds(r):
        for n in range(2):
            r[0](n).wait_recv()
        for n in range(2):
            r[1](n).start()

    def finished(r):
        for n in range(2):
            r[1](n).wait_recv()

    firsts(down_ring)
    firsts(up_rings[0])
    firsts(up_rings[1])

    def cross_step(i, _):
        step(0, i)

        @pl.when(i == 8)
        def _():
            pack(1)
            begin(1)

        @pl.when(i == 1)
        def _():
            seconds(down_ring)
            firsts(down_spread[0])
            firsts(down_spread[1])

        @pl.when(i == 10)
        def _():
            mine = lines.at[rows16(32 * c, 32)]
            pltpu.make_async_copy(mine, mine, t_r).wait()
            l_copy().start()

        @pl.when(i >= STEPS - 15)
        def _():
            step(1, i - STEPS + 15)

        return 0

    lax.fori_loop(0, STEPS - 12, cross_step, 0)
    loads[0].wait()
    loads[1].wait()
    theirs = lines.at[rows16(32 * (1 - c), 32)]
    rcopy(theirs, theirs, i_s, i_r, gx, gz).wait_recv()
    which = which_axis((XL, D))
    pos = jnp.where(
        which == 1, enc[...], jnp.where(which == 0, enc[pl.ds(inl, 1), :], enc[pl.ds(dep, 1), :])
    )
    nbuf[...] = normed(lines[...].astype(F32).reshape(XL, D) + pos, gains[0:1, :])
    q = lax.broadcasted_iota(jnp.int32, (MINE, XL), 0)
    r = lax.broadcasted_iota(jnp.int32, (MINE, XL), 1)
    pick = jnp.where(r == 4 * (q // 2) + 2 * c + q % 2, 1.0, 0.0).astype(BF)
    nown[...] = jnp.dot(pick, nbuf[...], preferred_element_type=F32).astype(BF)

    lax.fori_loop(STEPS - 12, STEPS, cross_step, 0)

    def attend(base, keys_in, queries_in, count, mask, between):
        def project(part, tokens_in, left):
            a, b = (w[k, base + part * D : base + (part + 1) * D, :] for k in range(2))
            lo, hi = tokens_in[:, :HALF], tokens_in[:, HALF:]
            return (nt(a, lo) + nt(b, hi) if left else nt(lo, a) + nt(hi, b)).astype(BF)

        qbuf[...] = project(0, queries_in, True)
        kbuf[0:count, :] = project(1, keys_in, False)
        vbuf[:, 0:count] = project(2, keys_in, True)

        def two(p, _):
            keys = kbuf[0:count, pl.ds(pl.multiple_of(128 * p, 128), 128)]
            for j in range(2):
                at = rows16(128 * p + HDIM * j, HDIM)
                scores = jnp.dot(
                    keys[:, HDIM * j : HDIM * (j + 1)], qbuf[at, :], preferred_element_type=F32
                ) * (HDIM**-0.5)
                if mask is not None:
                    scores = jnp.where(mask, scores, -1e30)
                expo = jnp.exp(scores - jnp.max(scores, 0, keepdims=True))
                total = jnp.sum(expo, 0, keepdims=True)
                obuf[at, :] = (
                    jnp.dot(vbuf[at, 0:count], expo.astype(BF), preferred_element_type=F32) / total
                )
            if between:
                between(p)
            return 0

        lax.fori_loop(0, HEADS // 2, two, 0)

    siblings(0)

    def depth_step(i, _):
        step(1, i)
        return 0

    attend(0, nbuf, nown, XL, None, lambda p: lax.fori_loop(15 + 2 * p, 17 + 2 * p, depth_step, 0))
    sendb[...] = obuf[...].T.reshape(GX, 2, D).astype(BF)

    def k_copy(i):
        return rcopy(sendb.at[i], mixed.at[dep], k_s.at[i], k_r, i, 2 * inl + c)

    def k_start(i, _):
        here = jnp.logical_and(i == gx, me_too)

        @pl.when(jnp.logical_not(here))
        def _():
            k_copy(i).start()

        @pl.when(here)
        def _():
            pltpu.make_async_copy(sendb.at[i], mixed.at[dep], k_r).start()

        return 0

    lax.fori_loop(0, 64, k_start, 0)

    finished(down_ring)
    firsts(down_spread[2])
    seconds(up_rings[0])
    seconds(down_spread[0])
    seconds(down_spread[1])
    lax.fori_loop(27, STEPS, depth_step, 0)

    seconds(up_rings[1])
    seconds(down_spread[2])

    own_c.wait()
    for d in range(1, 8):
        c_copy(d).wait_recv()
    which = which_axis((MINE, D))
    odd = lax.broadcasted_iota(jnp.int32, (MINE, D), 0) % 2
    first = XLD * gx + 2 * c
    cross = jnp.where(odd == 0, enc[pl.ds(first, 1), :], enc[pl.ds(first + 1, 1), :])
    pos = jnp.where(which == 1, cross, jnp.where(which == 0, enc[pl.ds(x, 1), :], dep2[...]))
    stream = jnp.transpose(cols[...].astype(F32), (0, 2, 1, 3)).reshape(MINE, D) + pos

    def project_out(v, base):
        return jnp.concatenate(
            [
                jnp.dot(v, w[k, base : base + D, :], preferred_element_type=F32)
                for k in range(2)
            ],
            1,
        )

    pltpu.make_async_copy(mixed, mixed, k_r).wait()
    stream = stream + project_out(mixed[...].reshape(MINE, D), QKV)
    nown[...] = normed(stream, gains[1:2, :])
    mask = (
        lax.broadcasted_iota(jnp.int32, (MINE, MINE), 0)
        + lax.broadcasted_iota(jnp.int32, (MINE, MINE), 1)
    ) % 2 == 0
    siblings(1)
    attend(SPAN, nown, nown, MINE, mask, None)
    stream = stream + project_out(obuf[...].T.astype(BF), SPAN + QKV)
    nown[...] = normed(stream, gains[2:3, :])

    def tok_copy():
        return rcopy(nown, pairtok.at[c], a_s.at[0], a_r.at[0], gx, sib)

    def sum_copy():
        return rcopy(sent, pair, a_s.at[1], a_r.at[1], gx, sib)

    tok_copy().start()
    pairtok[c] = nown[...]
    loads[2].wait()
    loads[3].wait()
    there = pairtok.at[1 - c]
    rcopy(there, there, a_s.at[0], a_r.at[0], gx, gz).wait_recv()

    def hidden_part(k):
        both = pairtok[...].reshape(2 * MINE, D)
        hidden = jax.nn.gelu(jnp.dot(both, up[k], preferred_element_type=F32)).astype(BF)
        return jnp.dot(hidden, down[k], preferred_element_type=F32)

    for r in (*up_rings, *down_spread):
        finished(r)
    acc[...] = hidden_part(0) + hidden_part(1) + hidden_part(2) + hidden_part(3)
    sent[...] = acc[pl.ds(pl.multiple_of(MINE * (1 - c), MINE), MINE), :].astype(BF)
    sum_copy().start()
    stream = stream + acc[pl.ds(pl.multiple_of(MINE * c, MINE), MINE), :]
    sum_copy().wait_recv()
    stream = stream + pair[...].astype(F32)

    fbuf[...] = stream.astype(BF)

    def f_copy(d):
        there = (gz + d) % GZ
        return rcopy(fbuf.at[rows16(16 * there, 16)], frecv.at[gz], f_s.at[d - 1], f_r.at[d - 1], gx, there)

    own_f = pltpu.make_async_copy(fbuf.at[rows16(16 * gz, 16)], frecv.at[gz], l_s.at[11])
    own_f.start()
    for d in range(1, 8):
        f_copy(d).start()
    thick = jax.nn.softplus(jnp.sum(stream * head_w[...].reshape(1, D), -1, keepdims=True) + head_b[0])
    i = lax.broadcasted_iota(jnp.int32, (MINE, MINE), 0)
    j = lax.broadcasted_iota(jnp.int32, (MINE, MINE), 1)
    across = jnp.broadcast_to(thick, (MINE, MINE)).T
    keep = jnp.logical_and(j <= i, (i + j) % 2 == 0)
    line = jnp.sum(jnp.where(keep, across, 0.0), 1, keepdims=True)
    gbuf[...] = jnp.broadcast_to(line, (MINE, 128))

    def h_copy(d):
        there = (gz + d) % GZ
        return rcopy(gbuf.at[rows16(16 * there, 16)], trecv.at[gz], h_s.at[d - 1], h_r.at[d - 1], gx, there)

    own_h = pltpu.make_async_copy(gbuf.at[rows16(16 * gz, 16)], trecv.at[gz], l_s.at[12])
    own_h.start()
    for d in range(1, 8):
        h_copy(d).start()
    for d in range(1, 4):
        y_copy(0, d).wait_send()
        y_copy(1, d).wait_send()
    for d in range(1, 8):
        c_copy(d).wait_send()

    def t_end(i, _):
        @pl.when(jnp.logical_not(jnp.logical_and(32 * c + i == gx, own_line)))
        def _():
            t_copy(i).wait_send()

        return 0

    lax.fori_loop(0, 32, t_end, 0)

    def k_end(i, _):
        @pl.when(jnp.logical_not(jnp.logical_and(i == gx, me_too)))
        def _():
            k_copy(i).wait_send()

        return 0

    lax.fori_loop(0, 64, k_end, 0)
    l_copy().wait_send()
    for kind in range(2):
        @pl.when(seat(z) < 3)
        def _():
            for d in range(1, ZN):
                z_copy(kind, d).wait_send()

        def w_end(k, _):
            zsrc = (z + k) % ZN

            @pl.when(k > 0)
            def _():
                @pl.when(seat(zsrc) < 3)
                def _():
                    for d in range(1, 4):
                        x_copy(kind, zsrc, d).wait_send()

                for cp in spread(kind, zsrc):
                    cp.wait_send()
                onward(kind, zsrc).wait_send()

            for cp in relay(kind, zsrc):
                cp.wait_send()
            return 0

        lax.fori_loop(0, ZN, w_end, 0)
    for r in all_rings:
        for n in range(2):
            r[0](n).wait_send()
            r[1](n).wait_send()
    tok_copy().wait_send()
    sum_copy().wait_send()
    own_f.wait()
    for d in range(1, 8):
        f_copy(d).wait_recv()
    feat[...] = (
        jnp.transpose(frecv[...].astype(F32).reshape(GZ, DPD, 2, D), (0, 2, 1, 3))
        .reshape(INL, XLD, DPD, D)
        .astype(BF)
    )
    own_h.wait()
    for d in range(1, 8):
        h_copy(d).wait_recv()
    row = lax.broadcasted_iota(jnp.int32, (GZ, 16, 128), 1)
    lane = lax.broadcasted_iota(jnp.int32, (GZ, 16, 128), 2)
    for k in range(2):
        mark = jnp.logical_and(row // 2 == lane, row % 2 == k)
        picked = jnp.sum(jnp.where(mark, trecv[...], 0.0), 1)
        for n in range(GZ):
            time[n // 2, 2 * (n % 2) + k : 2 * (n % 2) + k + 1, :] = picked[n : n + 1, :DPD]
    for d in range(1, 8):
        f_copy(d).wait_send()
        h_copy(d).wait_send()


def body(
    tokens, cross_qkv, cross_out, depth_qkv, depth_out, up_proj, down_proj, gains, head_weight, head_bias
):
    enc = table()
    dep2 = jnp.asarray(np.repeat(enc[:DP], 2, 0))
    enc = jnp.asarray(enc)
    dma = pltpu.SemaphoreType.DMA
    vmem = pltpu.VMEM
    return pl.pallas_call(
        block_kernel,
        out_shape=(
            jax.ShapeDtypeStruct((INL, XLD, DPD, D), BF),
            jax.ShapeDtypeStruct((INL, XLD, DPD), F32),
        ),
        in_specs=[VM] * 7 + [pl.BlockSpec(memory_space=pltpu.SMEM), VM] + [ANY] * 4,
        out_specs=(VM, VM),
        scratch_shapes=[
            vmem((XL, D), F32),
            vmem((MINE, D), F32),
            vmem((XN, D, FF // GZ), BF),
            vmem((XN, FF // GZ, D), BF),
            vmem((SLOT, D), F32),
            vmem((2, 2, SLOT, HALF), BF),
            vmem((2, SLOT, HALF), BF),
            vmem((2, YN, SLOT, HALF), BF),
            vmem((BLOCK, HALF), BF),
            vmem((2, 2 * SPAN, HALF), BF),
            vmem((LINES, XLD, D), BF),
            vmem((GX, XLD, D), BF),
            vmem((GZ, 2, DPD, D), BF),
            vmem((XL, D), BF),
            vmem((XL, D), BF),
            vmem((D, MINE), BF),
            vmem((D, XL), BF),
            vmem((D, MINE), F32),
            vmem((GX, 2, D), BF),
            vmem((DP, 2, D), BF),
            vmem((MINE, D), BF),
            vmem((2, MINE, D), BF),
            vmem((2 * MINE, D), F32),
            vmem((MINE, D), BF),
            vmem((MINE, D), BF),
            vmem((MINE, D), BF),
            vmem((MINE, 128), F32),
            vmem((GZ, 16, D), BF),
            vmem((GZ, 16, 128), F32),
            dma((2, 3)), dma((2, 3)),
            dma((32,)), dma,
            dma((7,)), dma((7,)),
            dma((2, 15)), dma((2, 15)),
            dma((2, ZN, 3)), dma((2, ZN, 3)),
            dma((2, ZN, 3)), dma((2, ZN, 3)),
            dma((2, ZN, 2)), dma((2, ZN, 2)),
            dma, dma,
            dma((64,)), dma,
            dma((6, 4)), dma((6, 4)),
            dma((2,)), dma((2,)),
            dma((7,)), dma((7,)),
            dma((7,)), dma((7,)),
            dma((13,)),
        ],
        compiler_params=pltpu.CompilerParams(
            collective_id=0, has_side_effects=True, vmem_limit_bytes=LIMIT
        ),
        name="axial_block",
    )(
        tokens, cross_qkv.T, cross_out, depth_qkv.T, depth_out, gains, head_weight, head_bias,
        jnp.asarray(packing(), BF), enc, dep2, up_proj, down_proj,
    )


def solution(mesh):
    return jax.shard_map(
        body,
        mesh=mesh,
        in_specs=(
            P(None, "gx", "gz", None),
            P(None, "gx"),
            P("gx", None),
            P(None, "gx"),
            P("gx", None),
            P(None, "gz"),
            P("gz", None),
            P(),
            P(),
            P(),
        ),
        out_specs=(P(None, "gx", "gz", None), P(None, "gx", "gz")),
        check_vma=False,
    )
```
